512 devices in a mesh: row: 16 (over z_lo, core), col: 16 (over y, x), gz: 2 (over z_hi).
Axes of the slice: x: 4, y: 4, z: 16 (z_hi: 2, z_lo: 8; z = z_hi * 8 + z_lo), core: 2. Of those that a mesh axis runs over, the one named last changes fastest.
Arguments:
- modes: bfloat16 [64, 96, 32, 3, 2048], P('row', 'col', 'gz'), may hold values from -0.109375 to 0.109375
- blocks: float32 [8, 7, 3, 3], replicated, may hold values from -6 to 6
- material: int32 [64, 96, 32], P('row', 'col', 'gz'), may hold values from 0 to 7
Outputs:
- reduced: float32 [2048, 256], P('col')
The draws below stay inside these ranges and needn't reach their ends.
All inputs are finite; a program needn't handle non-finite values.
Results may differ from the reference program's by a relative error of at most 0.0029.
Values may be sent and summed in bfloat16 or wider, within the bound.
No kernel may reach another device: no remote copies, remote signals or barrier semaphores. Data moves between devices by JAX's collectives and lax.ppermute only.
A program may use at most 64 MiB of HBM per device.

```python
import jax
import jax.numpy as jnp
from jax import lax

FULL = 2048
PANEL = 256
NMAT = 8
NX = 64
NY = 96
NZ = 32


def place_ends(entries, stream_key, low, high):
    longest = entries.shape.index(max(entries.shape))
    spots = []
    for shift in (0, 1):
        where = [jax.random.randint(jax.random.fold_in(stream_key, axis), (), 0, length) for axis, length in enumerate(entries.shape)]
        where[longest] = (where[longest] + shift) % entries.shape[longest]
        spots.append(tuple(where))
    return entries.at[spots[0]].set(low).at[spots[1]].set(high)


def shard_levels(key, shape, cuts, smallest, high):
    factor_of, own = 1.0, jax.random.fold_in(key, 6)
    for axis_at, blocks in cuts:
        steps = jnp.exp(jax.random.uniform(jax.random.fold_in(own, axis_at), (blocks,), jnp.float32, smallest / len(cuts), high / len(cuts)))
        factor_of = factor_of * jnp.repeat(steps, shape[axis_at] // blocks).reshape([-1 if axis == axis_at else 1 for axis in range(len(shape))])
    return factor_of


def scatter_about(stream_key, shape, scale, reach, split=(), kind=jnp.bfloat16):
    loudness = shard_levels(stream_key, shape, split, -0.22, 0.18) if split else 1.0
    values = jax.random.normal(stream_key, shape, jnp.float32) * scale * loudness
    return jnp.minimum(jnp.maximum(values, -reach), reach).astype(kind)


def setup_inputs(seed: int = 0) -> dict:
    arg_keys = jax.random.split(jax.random.key(seed), 4)
    modes = scatter_about(arg_keys[0], (NX, NY, NZ, 3, FULL), ((63 * NX * NY * NZ) ** -0.25), 0.109375, ((0, 16), (1, 16), (2, 2)))
    blocks = scatter_about(arg_keys[1], (NMAT, 7, 3, 3), 1.0, 6.0, (), jnp.float32)
    material = place_ends(jax.random.randint(arg_keys[2], (NX, NY, NZ), 0, NMAT), jax.random.fold_in(arg_keys[2], 1), 0, NMAT - 1).astype(jnp.int32)
    return dict(modes=modes, blocks=blocks, material=material)


def couplings(material, blocks):
    kinds = jnp.arange(NMAT, dtype=jnp.int32)
    onehot = (material[..., None] == kinds).astype(jnp.float32)
    table = blocks.reshape(NMAT, 63)
    flat = jnp.einsum("xyzm,mk->xyzk", onehot, table, precision=lax.Precision.HIGHEST)
    return flat.reshape(material.shape + (7, 3, 3))


def neighbours(padded):
    centre = padded[1:-1, 1:-1, 1:-1]
    return [centre,
            padded[2:, 1:-1, 1:-1], padded[:-2, 1:-1, 1:-1],
            padded[1:-1, 2:, 1:-1], padded[1:-1, :-2, 1:-1],
            padded[1:-1, 1:-1, 2:], padded[1:-1, 1:-1, :-2]]


def apply_blocks(padded, coupling):
    pieces = neighbours(padded)
    result = jnp.zeros(pieces[0].shape, jnp.float32)
    for offset in range(7):
        result = result + jnp.einsum("xyzij,xyzjc->xyzic", coupling[:, :, :, offset], pieces[offset],
                                     precision=lax.Precision.HIGHEST)
    return result


def reference(modes, blocks, material):
    panel = modes[..., :PANEL].astype(jnp.float32)
    padded = jnp.pad(panel, ((1, 1), (1, 1), (1, 1), (0, 0), (0, 0)))
    coupling = couplings(material, blocks)
    stiff_panel = apply_blocks(padded, coupling).astype(jnp.bfloat16)
    slab_modes = modes.reshape(NX, NY * NZ * 3, FULL)
    slab_stiff = stiff_panel.reshape(NX, NY * NZ * 3, PANEL)

    def accumulate(carry, pair):
        left = pair[0].astype(jnp.float32)
        right = pair[1].astype(jnp.float32)
        carry = carry + lax.dot_general(left, right, (((0,), (0,)), ((), ())),
                                        precision=lax.Precision.HIGHEST)
        return carry, None

    start_value = jnp.zeros((FULL, PANEL), jnp.float32)
    reduced, unused = lax.scan(accumulate, start_value, (slab_modes, slab_stiff))
    return reduced
```

```python
import jax
import jax.numpy as jnp
from jax import lax
from jax.experimental import pallas as pl
from jax.experimental.pallas import tpu as pltpu
from jax.sharding import Mesh, PartitionSpec as P

PANEL = 256
HALF = 128
NMAT = 8
SX, SY, SZ = 4, 6, 16
CELLS = SX * SY
GROUP = 3 * SZ
ROWS = CELLS * GROUP
ROW, COL, GZ = ("z", "core"), ("y", "x"), "gz"
Z = ("gz", "z")
f32, bf16 = jnp.float32, jnp.bfloat16


def lane(values, k):
    return jnp.broadcast_to(values[:, k : k + 1], (values.shape[0], PANEL))


def local_kernel(kind_ref, table_ref, panel_ref, coef_ref, part_ref, grid_ref):
    table = table_ref[...]
    for n in range(CELLS):
        kind = jnp.broadcast_to(kind_ref[:, n : n + 1], (SZ, 128))
        coef = jnp.zeros((SZ, 128), f32)
        for m in range(NMAT):
            coef = jnp.where(kind == m, jnp.broadcast_to(table[m : m + 1, :], (SZ, 128)), coef)
        coef_ref[n] = coef
        x, y = divmod(n, SY)
        at = (x + 1) * (SY + 2) + y + 1
        grid_ref[at] = panel_ref[n * GROUP : (n + 1) * GROUP, :].astype(f32)
    zeros = jnp.zeros((GROUP, PANEL), f32)
    for y in range(SY + 2):
        grid_ref[y] = zeros
        grid_ref[(SX + 1) * (SY + 2) + y] = zeros
    for x in range(1, SX + 1):
        grid_ref[x * (SY + 2)] = zeros
        grid_ref[x * (SY + 2) + SY + 1] = zeros
    level = lax.broadcasted_iota(jnp.int32, (SZ, PANEL), 0)

    def cell(n, carry):
        at = (n // SY + 1) * (SY + 2) + n % SY + 1
        coef = coef_ref[n]
        total = [jnp.zeros((SZ, PANEL), f32) for _ in range(3)]
        sources = ((1, at + SY + 2), (2, at - SY - 2), (3, at + 1), (4, at - 1))
        for j in range(3):
            own = grid_ref[at, j * SZ : (j + 1) * SZ, :]
            above = jnp.where(level == SZ - 1, 0.0, pltpu.roll(own, SZ - 1, 0))
            below = jnp.where(level == 0, 0.0, pltpu.roll(own, 1, 0))
            terms = [(0, own), (5, above), (6, below)]
            terms += [(o, grid_ref[s, j * SZ : (j + 1) * SZ, :]) for o, s in sources]
            for o, value in terms:
                for i in range(3):
                    total[i] = total[i] + lane(coef, o * 9 + i * 3 + j) * value
        for i in range(3):
            start = pl.multiple_of(n * GROUP + i * SZ, SZ)
            part_ref[pl.ds(start, SZ), :] = total[i]
        return carry

    lax.fori_loop(0, CELLS, cell, 0)


def finish_kernel(coef_ref, part_ref, xlo_ref, xhi_ref, ylo_ref, yhi_ref, zface_ref, modes_ref,
                  keep_ref, send_ref, work_ref, stiff_ref):
    core, gz = lax.axis_index("core"), lax.axis_index("gz")
    level = lax.broadcasted_iota(jnp.int32, (SZ, 128), 0)
    edge = jnp.where(gz == 0, SZ - 1, 0)

    def face_z(n, carry):
        coef = coef_ref[n]
        mine = jnp.where(level == edge, jnp.where(gz == 0, coef, pltpu.roll(coef, 128 - 9, 1)), 0.0)
        rows = zface_ref[n].astype(f32)
        for i in range(3):
            start = pl.multiple_of(n * GROUP + i * SZ, SZ)
            total = part_ref[pl.ds(start, SZ), :]
            for j in range(3):
                total = total + lane(mine, 45 + i * 3 + j) * jnp.broadcast_to(rows[j : j + 1, :], (SZ, PANEL))
            work_ref[pl.ds(start, SZ), :] = total
        return carry

    lax.fori_loop(0, CELLS, face_z, 0)

    def face(n, o, ref, k):
        coef = coef_ref[n]
        for i in range(3):
            start = n * GROUP + i * SZ
            total = work_ref[start : start + SZ, :]
            for j in range(3):
                value = ref[k * GROUP + j * SZ : k * GROUP + (j + 1) * SZ, :].astype(f32)
                total = total + lane(coef, o * 9 + i * 3 + j) * value
            work_ref[start : start + SZ, :] = total

    for y in range(SY):
        face((SX - 1) * SY + y, 1, xhi_ref, y)
        face(y, 2, xlo_ref, y)
    for x in range(SX):
        face(x * SY + SY - 1, 3, yhi_ref, x)
        face(x * SY, 4, ylo_ref, x)
    stiff_ref[...] = work_ref[...].astype(bf16).T
    for t in range(modes_ref.shape[1] // PANEL):
        product = jnp.dot(stiff_ref[...], modes_ref[:, t * PANEL : (t + 1) * PANEL], preferred_element_type=f32)
        low, high = product[:HALF], product[HALF:]
        keep = jnp.where(core == 0, low, high)
        send = jnp.where(core == 0, high, low)
        for u in range(2):
            keep_ref[2 * t + u] = keep[:, u * HALF : (u + 1) * HALF]
            send_ref[2 * t + u] = send[:, u * HALF : (u + 1) * HALF]


def swap(value, axis):
    return lax.ppermute(value, axis, [(0, 1), (1, 0)])


def shards(modes, blocks, material):
    full = modes.shape[-1]
    grid = modes.transpose(0, 1, 3, 2, 4)
    panel = grid[..., :PANEL]
    chain = [(i, i + 1) for i in range(15)]
    back = [(j, i) for i, j in chain]
    gz = lax.axis_index(GZ)
    zsend = jnp.where(gz == 0, panel[:, :, :, SZ - 1], panel[:, :, :, 0]).reshape(CELLS, 3, PANEL)
    zface = swap(zsend, GZ)
    ylo = lax.ppermute(panel[:, SY - 1].reshape(-1, PANEL), COL, chain)
    yhi = lax.ppermute(panel[:, 0].reshape(-1, PANEL), COL, back)
    xlo = lax.ppermute(panel[SX - 1].reshape(-1, PANEL), ROW, chain)
    xhi = lax.ppermute(panel[0].reshape(-1, PANEL), ROW, back)
    kind = material.reshape(CELLS, SZ).T
    table = jnp.pad(blocks.reshape(NMAT, 63), ((0, 0), (0, 65)))
    flat = grid.reshape(ROWS, full)
    whole = lambda *shape: pl.BlockSpec(shape, lambda i: (0,) * len(shape))
    coef, part = pl.pallas_call(
        local_kernel,
        grid=(1,),
        in_specs=[whole(SZ, CELLS), whole(NMAT, 128), whole(ROWS, PANEL)],
        out_specs=[whole(CELLS, SZ, 128), whole(ROWS, PANEL)],
        out_shape=[jax.ShapeDtypeStruct((CELLS, SZ, 128), f32), jax.ShapeDtypeStruct((ROWS, PANEL), f32)],
        scratch_shapes=[pltpu.VMEM(((SX + 2) * (SY + 2), GROUP, PANEL), f32)],
        cost_estimate=pl.CostEstimate(flops=2 * ROWS * 21 * PANEL, bytes_accessed=3 * ROWS * PANEL, transcendentals=0),
        compiler_params=pltpu.CompilerParams(vmem_limit_bytes=24 << 20),
        name="local_stencil",
    )(kind, table, flat)
    tiles = full // HALF
    vmem = pl.BlockSpec(memory_space=pltpu.VMEM)
    keep, send = pl.pallas_call(
        finish_kernel,
        in_specs=[vmem] * 8,
        out_specs=[vmem] * 2,
        out_shape=[jax.ShapeDtypeStruct((tiles, HALF, HALF), f32)] * 2,
        scratch_shapes=[pltpu.VMEM((ROWS, PANEL), f32), pltpu.VMEM((PANEL, ROWS), bf16)],
        cost_estimate=pl.CostEstimate(flops=2 * ROWS * full * PANEL, bytes_accessed=2 * ROWS * full, transcendentals=0),
        compiler_params=pltpu.CompilerParams(vmem_limit_bytes=32 << 20),
        name="faces_and_product",
    )(coef, part, xlo, xhi, ylo, yhi, zface, flat)
    mine = (keep + swap(send, "core")).astype(bf16)
    parts = lax.all_to_all(mine, COL, 0, 0, tiled=True)
    plane = jnp.sum(parts.astype(f32), axis=0).astype(bf16)
    copies = jnp.broadcast_to(plane[None], (16,) + plane.shape)
    planes = lax.all_to_all(copies, Z, 0, 0, tiled=True)
    half = jnp.sum(planes.astype(f32), axis=0)
    other = swap(half, "core")
    core = lax.axis_index("core")
    both = jnp.where(core == 0, jnp.concatenate([half, other]), jnp.concatenate([other, half]))
    return both.T


def solution(mesh):
    split = Mesh(mesh.devices.reshape(8, 2, 4, 4, 2), ("z", "core", "y", "x", "gz"))
    return jax.shard_map(
        shards,
        mesh=split,
        in_specs=(P(ROW, COL, GZ, None, None), P(), P(ROW, COL, GZ)),
        out_specs=P(COL, None),
        check_vma=False,
    )
```

```python
import jax
import jax.numpy as jnp
from jax import lax
from jax.experimental import pallas as pl
from jax.experimental.pallas import tpu as pltpu
from jax.sharding import Mesh, PartitionSpec as P

PANEL = 256
HALF = 128
NMAT = 8
SX, SY, SZ = 4, 6, 16
CELLS = SX * SY
GROUP = 3 * SZ
ROWS = CELLS * GROUP
ROW, COL, GZ = ("zq", "zr", "core"), ("y", "x"), "gz"
Z = ("gz", "zq", "zr")
f32, bf16 = jnp.float32, jnp.bfloat16


def lane(values, o, i, j):
    k = (3 * i + j) * 7 + o
    return jnp.broadcast_to(values[:, k : k + 1], (values.shape[0], PANEL))


def collect_kernel(modes_ref, panel_ref, z_ref, xlo_ref, xhi_ref, ylo_ref, yhi_ref, raw_ref, split_ref, sem):
    copy = pltpu.make_async_copy(modes_ref.at[:, :PANEL], raw_ref, sem)
    copy.start()
    copy.wait()
    panel_ref[...] = raw_ref[...].astype(f32)
    first = jnp.where(lax.axis_index(GZ) == 0, SZ - 1, 0)
    for h in range(2):
        part = slice(h * HALF, (h + 1) * HALF)
        split_ref[h] = raw_ref[:, part].astype(f32)
        z_ref[:, part] = split_ref.at[h][pl.ds(first, 3 * CELLS, stride=SZ), :].astype(bf16)
    side = SY * GROUP
    xlo_ref[...] = raw_ref[:side, :]
    xhi_ref[...] = raw_ref[ROWS - side :, :]
    for x in range(SX):
        ylo_ref[x * GROUP : (x + 1) * GROUP, :] = raw_ref[x * side : x * side + GROUP, :]
        yhi_ref[x * GROUP : (x + 1) * GROUP, :] = raw_ref[(x + 1) * side - GROUP : (x + 1) * side, :]


def local_kernel(kind_ref, blocks_ref, panel_ref, coef_ref, part_ref, inner_ref, table_ref):
    table_ref[...] = jnp.zeros((NMAT, 128), f32)
    for i in range(3):
        for j in range(3):
            k = (3 * i + j) * 7
            table_ref[:, k : k + 7] = blocks_ref[i, j]
    table = table_ref[...]
    offset = lax.broadcasted_iota(jnp.int32, (SZ, 128), 1) % 7
    kinds = jnp.concatenate([kind_ref[y] for y in range(SY)]).astype(f32).T
    for n in range(CELLS):
        x, y = divmod(n, SY)
        kind = jnp.broadcast_to(kinds[:, y * SX + x : y * SX + x + 1], (SZ, 128))
        coef = jnp.zeros((SZ, 128), f32)
        for m in range(NMAT):
            coef = jnp.where(kind == m, jnp.broadcast_to(table[m : m + 1, :], (SZ, 128)), coef)
        coef_ref[n] = coef
        outside = [o for o, at in ((1, x == SX - 1), (2, x == 0), (3, y == SY - 1), (4, y == 0)) if at]
        for o in outside:
            coef = jnp.where(offset == o, 0.0, coef)
        inner_ref[n] = coef
    level = lax.broadcasted_iota(jnp.int32, (SZ, PANEL), 0)

    def cell(n, carry):
        coef = inner_ref[n]
        total = [jnp.zeros((SZ, PANEL), f32) for _ in range(3)]
        last = CELLS - 1
        sources = (
            (1, jnp.minimum(n + SY, last)),
            (2, jnp.maximum(n - SY, 0)),
            (3, jnp.minimum(n + 1, last)),
            (4, jnp.maximum(n - 1, 0)),
        )

        def rows(at, j):
            return panel_ref[pl.ds(pl.multiple_of(at * GROUP + j * SZ, SZ), SZ), :]

        for j in range(3):
            own = rows(n, j)
            above = jnp.where(level == SZ - 1, 0.0, pltpu.roll(own, SZ - 1, 0))
            below = jnp.where(level == 0, 0.0, pltpu.roll(own, 1, 0))
            terms = [(0, own), (5, above), (6, below)] + [(o, rows(at, j)) for o, at in sources]
            for o, value in terms:
                for i in range(3):
                    total[i] = total[i] + lane(coef, o, i, j) * value
        for i in range(3):
            part_ref[pl.ds(pl.multiple_of(n * GROUP + i * SZ, SZ), SZ), :] = total[i]
        return carry

    lax.fori_loop(0, CELLS, cell, 0)


def finish_kernel(zface_ref, ylo_ref, yhi_ref, xlo_ref, xhi_ref, coef_ref, part_ref, modes_ref,
                  keep_ref, send_ref, work_ref, stiff_ref, zrow_ref):
    zrow_ref[...] = zface_ref[...].astype(f32)
    core, gz = lax.axis_index("core"), lax.axis_index("gz")
    level = lax.broadcasted_iota(jnp.int32, (SZ, 128), 0)
    edge = jnp.where(gz == 0, SZ - 1, 0)

    def face_z(n, carry):
        coef = coef_ref[n]
        mine = jnp.where(level == edge, jnp.where(gz == 0, coef, pltpu.roll(coef, 127, 1)), 0.0)
        for i in range(3):
            start = pl.multiple_of(n * GROUP + i * SZ, SZ)
            total = part_ref[pl.ds(start, SZ), :]
            for j in range(3):
                total = total + lane(mine, 5, i, j) * jnp.broadcast_to(zrow_ref[pl.ds(3 * n + j, 1), :], (SZ, PANEL))
            work_ref[pl.ds(start, SZ), :] = total
        return carry

    lax.fori_loop(0, CELLS, face_z, 0)

    def face(n, o, ref, k):
        coef = coef_ref[n]
        for i in range(3):
            start = n * GROUP + i * SZ
            total = work_ref[start : start + SZ, :]
            for j in range(3):
                value = ref[k * GROUP + j * SZ : k * GROUP + (j + 1) * SZ, :].astype(f32)
                total = total + lane(coef, o, i, j) * value
            work_ref[start : start + SZ, :] = total

    for y in range(SY):
        face((SX - 1) * SY + y, 1, xhi_ref, y)
        face(y, 2, xlo_ref, y)
    for x in range(SX):
        face(x * SY + SY - 1, 3, yhi_ref, x)
        face(x * SY, 4, ylo_ref, x)
    stiff_ref[...] = work_ref[...].astype(bf16).T
    for t in range(modes_ref.shape[1] // PANEL):
        product = jnp.dot(stiff_ref[...], modes_ref[:, t * PANEL : (t + 1) * PANEL], preferred_element_type=f32)
        low, high = product[:HALF], product[HALF:]
        keep = jnp.where(core == 0, low, high)
        send = jnp.where(core == 0, high, low).astype(bf16)
        for u in range(2):
            keep_ref[2 * t + u] = keep[:, u * HALF : (u + 1) * HALF]
            send_ref[2 * t + u] = send[:, u * HALF : (u + 1) * HALF]


def fold_kernel(planes_ref, half_ref):
    for r in range(4):
        total = planes_ref[r]
        for q in range(1, 4):
            total = total + planes_ref[4 * q + r]
        half_ref[:, 32 * r : 32 * (r + 1)] = total.T


def swap(value, axis):
    return lax.ppermute(value, axis, [(0, 1), (1, 0)])


def shards(modes, blocks, material):
    full = modes.shape[-1]
    flat = modes.transpose(0, 1, 3, 2, 4).reshape(ROWS, full)
    chain = [(i, i + 1) for i in range(15)]
    back = [(j, i) for i, j in chain]
    vmem = pl.BlockSpec(memory_space=pltpu.VMEM)
    shape = jax.ShapeDtypeStruct
    xside, yside = SY * GROUP, SX * GROUP
    panel, zsend, xfirst, xlast, yfirst, ylast = pl.pallas_call(
        collect_kernel,
        in_specs=[pl.BlockSpec(memory_space=pl.ANY)],
        out_specs=[vmem] * 6,
        out_shape=[shape((ROWS, PANEL), f32)]
        + [shape((rows, PANEL), bf16) for rows in (3 * CELLS, xside, xside, yside, yside)],
        scratch_shapes=[pltpu.VMEM((ROWS, PANEL), bf16), pltpu.VMEM((2, ROWS, HALF), f32), pltpu.SemaphoreType.DMA],
        compiler_params=pltpu.CompilerParams(vmem_limit_bytes=57 << 20),
        name="collect_faces",
    )(flat)
    zface = swap(zsend, GZ)
    ylo = lax.ppermute(ylast, COL, chain)
    yhi = lax.ppermute(yfirst, COL, back)
    xlo = lax.ppermute(xlast, ROW, chain)
    xhi = lax.ppermute(xfirst, ROW, back)
    coef, part = pl.pallas_call(
        local_kernel,
        in_specs=[vmem] * 3,
        out_specs=[vmem] * 2,
        out_shape=[shape((CELLS, SZ, 128), f32), shape((ROWS, PANEL), f32)],
        scratch_shapes=[pltpu.VMEM((CELLS, SZ, 128), f32), pltpu.VMEM((NMAT, 128), f32)],
        cost_estimate=pl.CostEstimate(flops=2 * ROWS * 21 * PANEL, bytes_accessed=3 * ROWS * PANEL, transcendentals=0),
        compiler_params=pltpu.CompilerParams(vmem_limit_bytes=24 << 20),
        name="local_stencil",
    )(material.transpose(1, 0, 2), blocks.transpose(2, 3, 0, 1), panel)
    tiles = full // HALF
    keep, send = pl.pallas_call(
        finish_kernel,
        in_specs=[vmem] * 8,
        out_specs=[vmem] * 2,
        out_shape=[shape((tiles, HALF, HALF), dtype) for dtype in (f32, bf16)],
        scratch_shapes=[pltpu.VMEM((ROWS, PANEL), f32), pltpu.VMEM((PANEL, ROWS), bf16), pltpu.VMEM((3 * CELLS, PANEL), f32)],
        cost_estimate=pl.CostEstimate(flops=2 * ROWS * full * PANEL, bytes_accessed=2 * ROWS * full, transcendentals=0),
        compiler_params=pltpu.CompilerParams(vmem_limit_bytes=32 << 20),
        name="faces_and_product",
    )(zface, ylo, yhi, xlo, xhi, coef, part, flat)
    mine = (keep + swap(send, "core").astype(f32)).astype(bf16)
    parts = lax.all_to_all(mine, COL, 0, 0, tiled=True)
    plane = jnp.sum(parts.astype(f32), axis=0).reshape(4, 32, HALF)
    near = jnp.sum(lax.all_to_all(plane, "zr", 0, 0, tiled=True), axis=0)
    copies = jnp.broadcast_to(near[None], (16,) + near.shape)
    planes = lax.all_to_all(copies, Z, 0, 0, tiled=True)
    half = pl.pallas_call(
        fold_kernel,
        in_specs=[vmem],
        out_specs=vmem,
        out_shape=shape((HALF, HALF), f32),
        name="fold",
    )(planes)
    other = swap(half, "core")
    first = lax.axis_index("core") == 0
    return jnp.concatenate([jnp.where(first, half, other), jnp.where(first, other, half)], axis=1)


def solution(mesh):
    split = Mesh(mesh.devices.reshape(2, 4, 2, 4, 4, 2), ("zq", "zr", "core", "y", "x", "gz"))
    return jax.shard_map(
        shards,
        mesh=split,
        in_specs=(P(ROW, COL, GZ, None, None), P(), P(ROW, COL, GZ)),
        out_specs=P(COL, None),
        check_vma=False,
    )
```

```python
import jax
import jax.numpy as jnp
from jax import lax
from jax.experimental import pallas as pl
from jax.experimental.pallas import tpu as pltpu
from jax.sharding import Mesh, PartitionSpec as P

PANEL = 256
HALF = 128
NMAT = 8
SX, SY, SZ = 4, 6, 16
CELLS = SX * SY
GROUP = 3 * SZ
ROWS = CELLS * GROUP
EDGE = 3 * CELLS
TALL = PANEL + 80
ROW, COL, GZ = ("zh", "zl", "core"), ("y", "x"), "gz"
Z = ("gz", "zh", "zl")
f32, bf16 = jnp.float32, jnp.bfloat16


def lane(values, o, i, j, width=PANEL):
    k = (3 * i + j) * 7 + o
    return jnp.broadcast_to(values[:, k : k + 1], (values.shape[0], width))


def collect_kernel(modes_ref, panel_ref, z_ref, xlo_ref, xhi_ref, ylo_ref, yhi_ref, raw_ref, split_ref, edge_ref, sem):
    copy = pltpu.make_async_copy(modes_ref.at[:, :PANEL], raw_ref, sem)
    copy.start()
    copy.wait()
    panel_ref[...] = raw_ref[...].astype(f32)
    first = jnp.where(lax.axis_index(GZ) == 0, SZ - 1, 0)
    for h in range(2):
        part = slice(h * HALF, (h + 1) * HALF)
        split_ref[h] = raw_ref[:, part].astype(f32)
        for j in range(3):
            rows = split_ref.at[h][pl.ds(j * SZ + first, CELLS, stride=GROUP), :]
            edge_ref[j * CELLS : (j + 1) * CELLS, part] = rows
    z_ref[...] = edge_ref[...].astype(bf16)
    side = SY * GROUP
    xlo_ref[...] = raw_ref[:side, :]
    xhi_ref[...] = raw_ref[ROWS - side :, :]
    for x in range(SX):
        ylo_ref[x * GROUP : (x + 1) * GROUP, :] = raw_ref[x * side : x * side + GROUP, :]
        yhi_ref[x * GROUP : (x + 1) * GROUP, :] = raw_ref[(x + 1) * side - GROUP : (x + 1) * side, :]


def local_kernel(kind_ref, blocks_ref, panel_ref, coef_ref, part_ref, inner_ref, table_ref):
    table_ref[...] = jnp.zeros((NMAT, 128), f32)
    for i in range(3):
        for j in range(3):
            k = (3 * i + j) * 7
            table_ref[:, k : k + 7] = blocks_ref[i, j]
    table = table_ref[...]
    offset = lax.broadcasted_iota(jnp.int32, (SZ, 128), 1) % 7
    kinds = jnp.concatenate([kind_ref[y] for y in range(SY)]).astype(f32).T
    for n in range(CELLS):
        x, y = divmod(n, SY)
        kind = jnp.broadcast_to(kinds[:, y * SX + x : y * SX + x + 1], (SZ, 128))
        coef = jnp.zeros((SZ, 128), f32)
        for m in range(NMAT):
            coef = jnp.where(kind == m, jnp.broadcast_to(table[m : m + 1, :], (SZ, 128)), coef)
        coef_ref[n] = coef
        outside = [o for o, at in ((1, x == SX - 1), (2, x == 0), (3, y == SY - 1), (4, y == 0)) if at]
        for o in outside:
            coef = jnp.where(offset == o, 0.0, coef)
        inner_ref[n] = coef
    level = lax.broadcasted_iota(jnp.int32, (SZ, PANEL), 0)

    def cell(n, carry):
        coef = inner_ref[n]
        total = [jnp.zeros((SZ, PANEL), f32) for _ in range(3)]
        last = CELLS - 1
        sources = (
            (1, jnp.minimum(n + SY, last)),
            (2, jnp.maximum(n - SY, 0)),
            (3, jnp.minimum(n + 1, last)),
            (4, jnp.maximum(n - 1, 0)),
        )

        def rows(at, j):
            return panel_ref[pl.ds(pl.multiple_of(at * GROUP + j * SZ, SZ), SZ), :]

        for j in range(3):
            own = rows(n, j)
            above = jnp.where(level == SZ - 1, 0.0, pltpu.roll(own, SZ - 1, 0))
            below = jnp.where(level == 0, 0.0, pltpu.roll(own, 1, 0))
            terms = [(0, own), (5, above), (6, below)] + [(o, rows(at, j)) for o, at in sources]
            for o, value in terms:
                for i in range(3):
                    total[i] = total[i] + lane(coef, o, i, j) * value
        for i in range(3):
            part_ref[pl.ds(pl.multiple_of(n * GROUP + i * SZ, SZ), SZ), :] = total[i]
        return carry

    lax.fori_loop(0, CELLS, cell, 0)


def product_kernel(ylo_ref, yhi_ref, xlo_ref, xhi_ref, coef_ref, part_ref, modes_ref,
                   sum_ref, edge_ref, edge_modes_ref, edge_coef_ref, stiff_ref, left_ref):
    gz = lax.axis_index(GZ)
    edge = jnp.where(gz == 0, SZ - 1, 0)
    level = lax.broadcasted_iota(jnp.int32, (SZ, PANEL), 0)
    for n in range(CELLS):
        x, y = divmod(n, SY)
        coef = coef_ref[n * SZ : (n + 1) * SZ, :]
        faces = [(1, xhi_ref, y)] if x == SX - 1 else []
        faces += [(2, xlo_ref, y)] if x == 0 else []
        faces += [(3, yhi_ref, x)] if y == SY - 1 else []
        faces += [(4, ylo_ref, x)] if y == 0 else []
        for i in range(3):
            start = n * GROUP + i * SZ
            total = part_ref[start : start + SZ, :]
            for o, ref, k in faces:
                for j in range(3):
                    value = ref[k * GROUP + j * SZ : k * GROUP + (j + 1) * SZ, :].astype(f32)
                    total = total + lane(coef, o, i, j) * value
            row = i * CELLS + n
            edge_ref[row : row + 1, :] = jnp.where(gz == 0, total[SZ - 1 :], total[:1])
            stiff_ref[start : start + SZ, :] = jnp.where(level == edge, 0.0, total).astype(bf16)
    left_ref[:PANEL, :] = stiff_ref[...].T
    row = lax.broadcasted_iota(jnp.int32, (TALL - PANEL, ROWS), 0)
    column = lax.broadcasted_iota(jnp.int32, (TALL - PANEL, ROWS), 1)
    target = (row % CELLS) * GROUP + (row // CELLS) * SZ + edge
    left_ref[PANEL:, :] = jnp.where((column == target) & (row < EDGE), 1.0, 0.0).astype(bf16)
    edge_coef_ref[...] = coef_ref[pl.ds(edge, CELLS, stride=SZ), :]
    for t in range(modes_ref.shape[1] // PANEL):
        part = slice(t * PANEL, (t + 1) * PANEL)
        product = jnp.dot(left_ref[...], modes_ref[:, part], preferred_element_type=f32)
        sum_ref[:, part] = product[:PANEL]
        edge_modes_ref[:, part] = product[PANEL:].astype(bf16)


def edge_kernel(zface_ref, sum_ref, edge_ref, edge_modes_ref, edge_coef_ref, keep_ref, send_ref, stiff_ref):
    core, gz = lax.axis_index("core"), lax.axis_index(GZ)
    coef = edge_coef_ref[...]
    coef = jnp.where(gz == 0, coef, pltpu.roll(coef, 127, 1))
    stiff_ref[...] = jnp.zeros(stiff_ref.shape, f32)
    for i in range(3):
        total = edge_ref[i * CELLS : (i + 1) * CELLS, :]
        for j in range(3):
            total = total + lane(coef, 5, i, j) * zface_ref[j * CELLS : (j + 1) * CELLS, :].astype(f32)
        stiff_ref[i * CELLS : (i + 1) * CELLS, :] = total
    left = stiff_ref[...].T.astype(bf16)
    for t in range(sum_ref.shape[1] // PANEL):
        part = slice(t * PANEL, (t + 1) * PANEL)
        product = sum_ref[:, part] + jnp.dot(left, edge_modes_ref[:, part], preferred_element_type=f32)
        low, high = product[:HALF], product[HALF:]
        keep = jnp.where(core == 0, low, high)
        send = jnp.where(core == 0, high, low).astype(bf16)
        for u in range(2):
            keep_ref[2 * t + u] = keep[:, u * HALF : (u + 1) * HALF]
            send_ref[2 * t + u] = send[:, u * HALF : (u + 1) * HALF]


def near_kernel(parts_ref, copies_ref):
    total = parts_ref[0].astype(f32)
    for k in range(1, parts_ref.shape[0]):
        total = total + parts_ref[k].astype(f32)
    total = total.astype(bf16)
    for k in range(copies_ref.shape[0]):
        copies_ref[k] = total


def fold_kernel(planes_ref, half_ref):
    for r in range(2):
        total = planes_ref[r].astype(f32)
        for q in range(1, 8):
            total = total + planes_ref[2 * q + r].astype(f32)
        half_ref[:, 64 * r : 64 * (r + 1)] = total.T


def swap(value, axis):
    return lax.ppermute(value, axis, [(0, 1), (1, 0)])


def shards(modes, blocks, material):
    full = modes.shape[-1]
    flat = modes.transpose(0, 1, 3, 2, 4).reshape(ROWS, full)
    chain = [(i, i + 1) for i in range(15)]
    back = [(j, i) for i, j in chain]
    vmem = pl.BlockSpec(memory_space=pltpu.VMEM)
    shape = jax.ShapeDtypeStruct
    xside, yside = SY * GROUP, SX * GROUP
    panel, zsend, xfirst, xlast, yfirst, ylast = pl.pallas_call(
        collect_kernel,
        in_specs=[pl.BlockSpec(memory_space=pl.ANY)],
        out_specs=[vmem] * 6,
        out_shape=[shape((ROWS, PANEL), f32)]
        + [shape((rows, PANEL), bf16) for rows in (3 * CELLS, xside, xside, yside, yside)],
        scratch_shapes=[pltpu.VMEM((ROWS, PANEL), bf16), pltpu.VMEM((2, ROWS, HALF), f32), pltpu.VMEM((EDGE, PANEL), f32), pltpu.SemaphoreType.DMA],
        compiler_params=pltpu.CompilerParams(vmem_limit_bytes=57 << 20),
        name="collect_faces",
    )(flat)
    zface = swap(zsend, GZ)
    ylo = lax.ppermute(ylast, COL, chain)
    yhi = lax.ppermute(yfirst, COL, back)
    xlo = lax.ppermute(xlast, ROW, chain)
    xhi = lax.ppermute(xfirst, ROW, back)
    coef, part = pl.pallas_call(
        local_kernel,
        in_specs=[vmem] * 3,
        out_specs=[vmem] * 2,
        out_shape=[shape((CELLS, SZ, 128), f32), shape((ROWS, PANEL), f32)],
        scratch_shapes=[pltpu.VMEM((CELLS, SZ, 128), f32), pltpu.VMEM((NMAT, 128), f32)],
        cost_estimate=pl.CostEstimate(flops=2 * ROWS * 21 * PANEL, bytes_accessed=3 * ROWS * PANEL, transcendentals=0),
        compiler_params=pltpu.CompilerParams(vmem_limit_bytes=24 << 20),
        name="local_stencil",
    )(material.transpose(1, 0, 2), blocks.transpose(2, 3, 0, 1), panel)
    tiles = full // HALF
    total, edge, edge_modes, edge_coef = pl.pallas_call(
        product_kernel,
        in_specs=[vmem] * 7,
        out_specs=[vmem] * 4,
        out_shape=[
            shape((PANEL, full), f32),
            shape((EDGE, PANEL), f32),
            shape((TALL - PANEL, full), bf16),
            shape((CELLS, 128), f32),
        ],
        scratch_shapes=[pltpu.VMEM((ROWS, PANEL), bf16), pltpu.VMEM((TALL, ROWS), bf16)],
        cost_estimate=pl.CostEstimate(flops=2 * ROWS * full * TALL, bytes_accessed=2 * ROWS * full, transcendentals=0),
        compiler_params=pltpu.CompilerParams(vmem_limit_bytes=32 << 20),
        name="faces_and_product",
    )(ylo, yhi, xlo, xhi, coef.reshape(CELLS * SZ, 128), part, flat)
    keep, send = pl.pallas_call(
        edge_kernel,
        in_specs=[vmem] * 5,
        out_specs=[vmem] * 2,
        out_shape=[shape((tiles, HALF, HALF), dtype) for dtype in (f32, bf16)],
        scratch_shapes=[pltpu.VMEM((TALL - PANEL, PANEL), f32)],
        cost_estimate=pl.CostEstimate(flops=2 * EDGE * full * PANEL, bytes_accessed=4 * PANEL * full, transcendentals=0),
        compiler_params=pltpu.CompilerParams(vmem_limit_bytes=24 << 20),
        name="edge_rows",
    )(zface, total, edge, edge_modes, edge_coef)
    mine = (keep + swap(send, "core").astype(f32)).astype(bf16)
    parts = lax.all_to_all(mine.reshape(2 * tiles, HALF // 2, HALF), COL + ("zl",), 0, 0, tiled=True)
    copies = pl.pallas_call(
        near_kernel,
        in_specs=[vmem],
        out_specs=vmem,
        out_shape=shape((16, HALF // 2, HALF), bf16),
        compiler_params=pltpu.CompilerParams(vmem_limit_bytes=4 << 20),
        name="near_sum",
    )(parts)
    planes = lax.all_to_all(copies, Z, 0, 0, tiled=True)
    half = pl.pallas_call(
        fold_kernel,
        in_specs=[vmem],
        out_specs=vmem,
        out_shape=shape((HALF, HALF), f32),
        compiler_params=pltpu.CompilerParams(vmem_limit_bytes=4 << 20),
        name="fold",
    )(planes)
    other = swap(half, "core")
    first = lax.axis_index("core") == 0
    return jnp.concatenate([jnp.where(first, half, other), jnp.where(first, other, half)], axis=1)


def solution(mesh):
    split = Mesh(mesh.devices.reshape(4, 2, 2, 4, 4, 2), ("zh", "zl", "core", "y", "x", "gz"))
    return jax.shard_map(
        shards,
        mesh=split,
        in_specs=(P(ROW, COL, GZ, None, None), P(), P(ROW, COL, GZ)),
        out_specs=P(COL, None),
        check_vma=False,
    )
```

```python
import jax
import jax.numpy as jnp
from jax import lax
from jax.experimental import pallas as pl
from jax.experimental.pallas import tpu as pltpu
from jax.sharding import Mesh, PartitionSpec as P

PANEL = 256
HALF = 128
NMAT = 8
SX, SY, SZ = 4, 6, 16
CELLS = SX * SY
GROUP = 3 * SZ
ROWS = CELLS * GROUP
EDGE = 3 * CELLS
ROW, COL, GZ = ("zh", "zl", "core"), ("y", "x"), "gz"
Z = ("gz", "zh", "zl")
f32, bf16 = jnp.float32, jnp.bfloat16


def lane(values, o, i, j, width=PANEL):
    k = (3 * i + j) * 7 + o
    return jnp.broadcast_to(values[:, k : k + 1], (values.shape[0], width))


def collect_kernel(modes_ref, panel_ref, z_ref, xlo_ref, xhi_ref, ylo_ref, yhi_ref, raw_ref, edge_ref, sem):
    copy = pltpu.make_async_copy(modes_ref.at[:, :PANEL], raw_ref, sem)
    copy.start()
    copy.wait()
    first = jnp.where(lax.axis_index(GZ) == 0, SZ - 1, 0)
    for h in range(2):
        part = slice(h * HALF, (h + 1) * HALF)
        panel_ref[h] = raw_ref[:, part].astype(f32)
        for j in range(3):
            rows = panel_ref.at[h][pl.ds(j * SZ + first, CELLS, stride=GROUP), :]
            edge_ref[j * CELLS : (j + 1) * CELLS, part] = rows
    z_ref[...] = edge_ref[...].astype(bf16)
    side = SY * GROUP
    xlo_ref[...] = raw_ref[:side, :]
    xhi_ref[...] = raw_ref[ROWS - side :, :]
    for x in range(SX):
        ylo_ref[x * GROUP : (x + 1) * GROUP, :] = raw_ref[x * side : x * side + GROUP, :]
        yhi_ref[x * GROUP : (x + 1) * GROUP, :] = raw_ref[(x + 1) * side - GROUP : (x + 1) * side, :]


def local_kernel(kind_ref, blocks_ref, panel_ref, modes_ref, coef_ref, part_ref, near_ref, inner_ref, table_ref, sem):
    copy = pltpu.make_async_copy(modes_ref, near_ref, sem)
    copy.start()
    table_ref[...] = jnp.zeros((NMAT, 128), f32)
    for i in range(3):
        for j in range(3):
            k = (3 * i + j) * 7
            table_ref[:, k : k + 7] = blocks_ref[i, j]
    table = table_ref[...]
    offset = lax.broadcasted_iota(jnp.int32, (SZ, 128), 1) % 7
    kinds = jnp.concatenate([kind_ref[y] for y in range(SY)]).astype(f32).T
    for n in range(CELLS):
        x, y = divmod(n, SY)
        kind = jnp.broadcast_to(kinds[:, y * SX + x : y * SX + x + 1], (SZ, 128))
        coef = jnp.zeros((SZ, 128), f32)
        for m in range(NMAT):
            coef = jnp.where(kind == m, jnp.broadcast_to(table[m : m + 1, :], (SZ, 128)), coef)
        coef_ref[n] = coef
        outside = [o for o, at in ((1, x == SX - 1), (2, x == 0), (3, y == SY - 1), (4, y == 0)) if at]
        for o in outside:
            coef = jnp.where(offset == o, 0.0, coef)
        inner_ref[n] = coef
    level = lax.broadcasted_iota(jnp.int32, (SZ, PANEL), 0)

    def cell(n, carry):
        coef = inner_ref[n]
        total = [jnp.zeros((SZ, PANEL), f32) for _ in range(3)]
        last = CELLS - 1
        sources = (
            (1, jnp.minimum(n + SY, last)),
            (2, jnp.maximum(n - SY, 0)),
            (3, jnp.minimum(n + 1, last)),
            (4, jnp.maximum(n - 1, 0)),
        )

        def rows(at, j):
            start = pl.multiple_of(at * GROUP + j * SZ, SZ)
            return jnp.concatenate([panel_ref[h, pl.ds(start, SZ), :] for h in range(2)], axis=1)

        for j in range(3):
            own = rows(n, j)
            above = jnp.where(level == SZ - 1, 0.0, pltpu.roll(own, SZ - 1, 0))
            below = jnp.where(level == 0, 0.0, pltpu.roll(own, 1, 0))
            terms = [(0, own), (5, above), (6, below)] + [(o, rows(at, j)) for o, at in sources]
            for o, value in terms:
                for i in range(3):
                    total[i] = total[i] + lane(coef, o, i, j) * value
        for i in range(3):
            part_ref[pl.ds(pl.multiple_of(n * GROUP + i * SZ, SZ), SZ), :] = total[i]
        return carry

    lax.fori_loop(0, CELLS, cell, 0)
    copy.wait()


def edge_kernel(zface_ref, coef_ref, term_ref):
    gz = lax.axis_index(GZ)
    coef = coef_ref[pl.ds(jnp.where(gz == 0, SZ - 1, 0), CELLS, stride=SZ), :]
    coef = jnp.where(gz == 0, coef, pltpu.roll(coef, 127, 1))
    for i in range(3):
        total = jnp.zeros((CELLS, PANEL), f32)
        for j in range(3):
            total = total + lane(coef, 5, i, j) * zface_ref[j * CELLS : (j + 1) * CELLS, :].astype(f32)
        term_ref[i * CELLS : (i + 1) * CELLS, :] = total


def product_kernel(ylo_ref, yhi_ref, xlo_ref, xhi_ref, coef_ref, part_ref, term_ref, modes_ref,
                   keep_ref, send_ref, stiff_ref, left_ref):
    core, gz = lax.axis_index("core"), lax.axis_index(GZ)
    level = lax.broadcasted_iota(jnp.int32, (SZ, PANEL), 0)
    at_edge = level == jnp.where(gz == 0, SZ - 1, 0)
    for n in range(CELLS):
        x, y = divmod(n, SY)
        coef = coef_ref[n * SZ : (n + 1) * SZ, :]
        faces = [(1, xhi_ref, y)] if x == SX - 1 else []
        faces += [(2, xlo_ref, y)] if x == 0 else []
        faces += [(3, yhi_ref, x)] if y == SY - 1 else []
        faces += [(4, ylo_ref, x)] if y == 0 else []
        for i in range(3):
            start = n * GROUP + i * SZ
            row = i * CELLS + n
            term = jnp.broadcast_to(term_ref[row : row + 1, :], (SZ, PANEL))
            total = part_ref[start : start + SZ, :] + jnp.where(at_edge, term, 0.0)
            for o, ref, k in faces:
                for j in range(3):
                    value = ref[k * GROUP + j * SZ : k * GROUP + (j + 1) * SZ, :].astype(f32)
                    total = total + lane(coef, o, i, j) * value
            stiff_ref[start : start + SZ, :] = total.astype(bf16)
    left_ref[...] = stiff_ref[...].T
    for t in range(modes_ref.shape[1] // PANEL):
        part = slice(t * PANEL, (t + 1) * PANEL)
        product = jnp.dot(left_ref[...], modes_ref[:, part], preferred_element_type=f32)
        low, high = product[:HALF], product[HALF:]
        keep = jnp.where(core == 0, low, high)
        send = jnp.where(core == 0, high, low).astype(bf16)
        for u in range(2):
            keep_ref[2 * t + u] = keep[:, u * HALF : (u + 1) * HALF]
            send_ref[2 * t + u] = send[:, u * HALF : (u + 1) * HALF]


def near_kernel(parts_ref, copies_ref):
    total = parts_ref[0].astype(f32)
    for k in range(1, parts_ref.shape[0]):
        total = total + parts_ref[k].astype(f32)
    total = total.astype(bf16)
    for k in range(copies_ref.shape[0]):
        copies_ref[k] = total


def fold_kernel(planes_ref, half_ref):
    for r in range(2):
        total = planes_ref[r].astype(f32)
        for q in range(1, 8):
            total = total + planes_ref[2 * q + r].astype(f32)
        half_ref[:, 64 * r : 64 * (r + 1)] = total.T


def swap(value, axis):
    return lax.ppermute(value, axis, [(0, 1), (1, 0)])


def shards(modes, blocks, material):
    full = modes.shape[-1]
    flat = modes.transpose(0, 1, 3, 2, 4).reshape(ROWS, full)
    chain = [(i, i + 1) for i in range(15)]
    back = [(j, i) for i, j in chain]
    vmem = pl.BlockSpec(memory_space=pltpu.VMEM)
    shape = jax.ShapeDtypeStruct
    xside, yside = SY * GROUP, SX * GROUP
    panel, zsend, xfirst, xlast, yfirst, ylast = pl.pallas_call(
        collect_kernel,
        in_specs=[pl.BlockSpec(memory_space=pl.ANY)],
        out_specs=[vmem] * 6,
        out_shape=[shape((2, ROWS, HALF), f32)]
        + [shape((rows, PANEL), bf16) for rows in (3 * CELLS, xside, xside, yside, yside)],
        scratch_shapes=[pltpu.VMEM((ROWS, PANEL), bf16), pltpu.VMEM((EDGE, PANEL), f32), pltpu.SemaphoreType.DMA],
        compiler_params=pltpu.CompilerParams(vmem_limit_bytes=50 << 20),
        name="collect_faces",
    )(flat)
    zface = swap(zsend, GZ)
    ylo = lax.ppermute(ylast, COL, chain)
    yhi = lax.ppermute(yfirst, COL, back)
    xlo = lax.ppermute(xlast, ROW, chain)
    xhi = lax.ppermute(xfirst, ROW, back)
    coef, part, near = pl.pallas_call(
        local_kernel,
        in_specs=[vmem] * 3 + [pl.BlockSpec(memory_space=pl.ANY)],
        out_specs=[vmem] * 3,
        out_shape=[shape((CELLS, SZ, 128), f32), shape((ROWS, PANEL), f32), shape((ROWS, full), bf16)],
        scratch_shapes=[pltpu.VMEM((CELLS, SZ, 128), f32), pltpu.VMEM((NMAT, 128), f32), pltpu.SemaphoreType.DMA],
        cost_estimate=pl.CostEstimate(flops=2 * ROWS * 21 * PANEL, bytes_accessed=3 * ROWS * PANEL, transcendentals=0),
        compiler_params=pltpu.CompilerParams(vmem_limit_bytes=46 << 20),
        name="local_stencil",
    )(material.transpose(1, 0, 2), blocks.transpose(2, 3, 0, 1), panel, flat)
    tiles = full // HALF
    coef = coef.reshape(CELLS * SZ, 128)
    term = pl.pallas_call(
        edge_kernel,
        in_specs=[vmem] * 2,
        out_specs=vmem,
        out_shape=shape((EDGE, PANEL), f32),
        cost_estimate=pl.CostEstimate(flops=4 * 10**9, bytes_accessed=EDGE * PANEL * 6, transcendentals=0),
        compiler_params=pltpu.CompilerParams(vmem_limit_bytes=8 << 20),
        name="edge_terms",
    )(zface, coef)
    keep, send = pl.pallas_call(
        product_kernel,
        in_specs=[vmem] * 8,
        out_specs=[vmem] * 2,
        out_shape=[shape((tiles, HALF, HALF), dtype) for dtype in (f32, bf16)],
        scratch_shapes=[pltpu.VMEM((ROWS, PANEL), bf16), pltpu.VMEM((PANEL, ROWS), bf16)],
        cost_estimate=pl.CostEstimate(flops=2 * ROWS * full * PANEL, bytes_accessed=2 * ROWS * full, transcendentals=0),
        compiler_params=pltpu.CompilerParams(vmem_limit_bytes=32 << 20),
        name="faces_and_product",
    )(ylo, yhi, xlo, xhi, coef, part, term, near)
    mine = (keep + swap(send, "core").astype(f32)).astype(bf16)
    parts = lax.all_to_all(mine.reshape(2 * tiles, HALF // 2, HALF), COL + ("zl",), 0, 0, tiled=True)
    copies = pl.pallas_call(
        near_kernel,
        in_specs=[vmem],
        out_specs=vmem,
        out_shape=shape((16, HALF // 2, HALF), bf16),
        compiler_params=pltpu.CompilerParams(vmem_limit_bytes=4 << 20),
        name="near_sum",
    )(parts)
    planes = lax.all_to_all(copies, Z, 0, 0, tiled=True)
    half = pl.pallas_call(
        fold_kernel,
        in_specs=[vmem],
        out_specs=vmem,
        out_shape=shape((HALF, HALF), f32),
        compiler_params=pltpu.CompilerParams(vmem_limit_bytes=4 << 20),
        name="fold",
    )(planes)
    other = swap(half, "core")
    first = lax.axis_index("core") == 0
    return jnp.concatenate([jnp.where(first, half, other), jnp.where(first, other, half)], axis=1)


def solution(mesh):
    split = Mesh(mesh.devices.reshape(4, 2, 2, 4, 4, 2), ("zh", "zl", "core", "y", "x", "gz"))
    return jax.shard_map(
        shards,
        mesh=split,
        in_specs=(P(ROW, COL, GZ, None, None), P(), P(ROW, COL, GZ)),
        out_specs=P(COL, None),
        check_vma=False,
    )
```

```python
import jax
import jax.numpy as jnp
from jax import lax
from jax.experimental import pallas as pl
from jax.experimental.pallas import tpu as pltpu
from jax.sharding import Mesh, PartitionSpec as P

PANEL = 256
HALF = 128
NMAT = 8
SX, SY, SZ = 4, 6, 16
CELLS = SX * SY
GROUP = 3 * SZ
ROWS = CELLS * GROUP
EDGE = 3 * CELLS
ROW, COL, GZ = ("zh", "zl", "core"), ("y", "x"), "gz"
Z = ("gz", "zh", "zl")
f32, bf16 = jnp.float32, jnp.bfloat16


def lane(values, o, i, j, width=PANEL):
    k = (3 * i + j) * 7 + o
    return jnp.broadcast_to(values[:, k : k + 1], (values.shape[0], width))


def collect_kernel(modes_ref, panel_ref, z_ref, xin_ref, xout_ref, ylo_ref, yhi_ref, raw_ref, edge_ref, sem):
    copy = pltpu.make_async_copy(modes_ref.at[:, :PANEL], raw_ref, sem)
    copy.start()
    copy.wait()
    first = jnp.where(lax.axis_index(GZ) == 0, SZ - 1, 0)
    for h in range(2):
        part = slice(h * HALF, (h + 1) * HALF)
        panel_ref[h] = raw_ref[:, part].astype(f32)
        for j in range(3):
            rows = panel_ref.at[h][pl.ds(j * SZ + first, CELLS, stride=GROUP), :]
            edge_ref[j * CELLS : (j + 1) * CELLS, part] = rows
    z_ref[...] = edge_ref[...].astype(bf16)
    side = SY * GROUP
    low = lax.axis_index("core") == 0
    xin_ref[...] = jnp.where(low, raw_ref[ROWS - side :, :], raw_ref[:side, :])
    xout_ref[...] = jnp.where(low, raw_ref[:side, :], raw_ref[ROWS - side :, :])
    for x in range(SX):
        ylo_ref[x * GROUP : (x + 1) * GROUP, :] = raw_ref[x * side : x * side + GROUP, :]
        yhi_ref[x * GROUP : (x + 1) * GROUP, :] = raw_ref[(x + 1) * side - GROUP : (x + 1) * side, :]


def split3(value):
    high = value.astype(bf16).astype(f32)
    mid = (value - high).astype(bf16).astype(f32)
    low = value - high - mid
    return jnp.concatenate([high, mid, low, jnp.zeros_like(value)]).astype(bf16)


def local_kernel(kind_ref, blocks_ref, panel_ref, modes_ref,
                 coef_ref, part_ref, near_ref, table_ref, wide_ref, hot_ref, plane_ref, sem):
    copy = pltpu.make_async_copy(modes_ref, near_ref, sem)
    copy.start()
    table_ref[...] = jnp.zeros((NMAT, 128), f32)
    for i in range(3):
        for j in range(3):
            k = 3 * i + j
            values = blocks_ref[i, j]
            table_ref[:, 7 * k : 7 * k + 7] = values
            for o in range(7):
                column = jnp.broadcast_to(values[:, o : o + 1], (NMAT, HALF))
                wide_ref[o, :, k * HALF : (k + 1) * HALF] = split3(column)
    kinds = jnp.concatenate([kind_ref[y] for y in range(SY)]).astype(f32).T
    slot = lax.broadcasted_iota(jnp.int32, (SZ, 4 * NMAT), 1)
    slot = jnp.where(slot < 3 * NMAT, slot % NMAT, -1).astype(f32)
    none = jnp.zeros((SZ, 4 * NMAT), bf16)
    for n in range(CELLS):
        x, y = divmod(n, SY)
        kind = jnp.broadcast_to(kinds[:, y * SX + x : y * SX + x + 1], (SZ, 4 * NMAT))
        hot = jnp.where(kind == slot, 1.0, 0.0).astype(bf16)
        outside = (False, x == SX - 1, x == 0, y == SY - 1, y == 0)
        for o in range(5):
            hot_ref[o, n * SZ : (n + 1) * SZ, :] = none if outside[o] else hot
    coef_ref[...] = jnp.dot(hot_ref[0], split3(table_ref[...]), preferred_element_type=f32)
    for o in range(7):
        plane_ref[o] = jnp.dot(hot_ref[o if o < 5 else 0], wide_ref[o], preferred_element_type=f32)
    level = lax.broadcasted_iota(jnp.int32, (SZ, HALF), 0)
    top, bottom = level == SZ - 1, level == 0

    def cell(n, carry):
        last = CELLS - 1
        sources = (
            (1, jnp.minimum(n + SY, last)),
            (2, jnp.maximum(n - SY, 0)),
            (3, jnp.minimum(n + 1, last)),
            (4, jnp.maximum(n - 1, 0)),
        )
        here = pl.ds(pl.multiple_of(n * SZ, SZ), SZ)
        total = [[jnp.zeros((SZ, HALF), f32) for _ in range(2)] for _ in range(3)]

        def rows(at, j):
            start = pl.multiple_of(at * GROUP + j * SZ, SZ)
            return [panel_ref[h, pl.ds(start, SZ), :] for h in range(2)]

        for j in range(3):
            own = rows(n, j)
            above = [jnp.where(top, 0.0, pltpu.roll(v, SZ - 1, 0)) for v in own]
            below = [jnp.where(bottom, 0.0, pltpu.roll(v, 1, 0)) for v in own]
            terms = [(0, own), (5, above), (6, below)] + [(o, rows(at, j)) for o, at in sources]
            for o, values in terms:
                for i in range(3):
                    k = 3 * i + j
                    factor = plane_ref[o, here, k * HALF : (k + 1) * HALF]
                    for h in range(2):
                        total[i][h] = total[i][h] + factor * values[h]
        for i in range(3):
            start = pl.multiple_of(n * GROUP + i * SZ, SZ)
            for h in range(2):
                part_ref[pl.ds(start, SZ), h * HALF : (h + 1) * HALF] = total[i][h]
        return carry

    lax.fori_loop(0, CELLS, cell, 0, unroll=2)
    copy.wait()


def edge_kernel(zface_ref, coef_ref, term_ref):
    gz = lax.axis_index(GZ)
    coef = coef_ref[pl.ds(jnp.where(gz == 0, SZ - 1, 0), CELLS, stride=SZ), :]
    coef = jnp.where(gz == 0, coef, pltpu.roll(coef, 127, 1))
    for i in range(3):
        total = jnp.zeros((CELLS, PANEL), f32)
        for j in range(3):
            total = total + lane(coef, 5, i, j) * zface_ref[j * CELLS : (j + 1) * CELLS, :].astype(f32)
        term_ref[i * CELLS : (i + 1) * CELLS, :] = total


def product_kernel(ylo_ref, yhi_ref, chip_ref, beside_ref, coef_ref, part_ref, term_ref, modes_ref,
                   keep_ref, send_ref, stiff_ref, left_ref):
    core, gz = lax.axis_index("core"), lax.axis_index(GZ)
    level = lax.broadcasted_iota(jnp.int32, (SZ, PANEL), 0)
    at_edge = level == jnp.where(gz == 0, SZ - 1, 0)
    low = core == 0
    for n in range(CELLS):
        x, y = divmod(n, SY)
        coef = coef_ref[n * SZ : (n + 1) * SZ, :]
        faces = [(1, (chip_ref, beside_ref), y)] if x == SX - 1 else []
        faces += [(2, (beside_ref, chip_ref), y)] if x == 0 else []
        faces += [(3, (yhi_ref,), x)] if y == SY - 1 else []
        faces += [(4, (ylo_ref,), x)] if y == 0 else []
        for i in range(3):
            start = n * GROUP + i * SZ
            row = i * CELLS + n
            term = jnp.broadcast_to(term_ref[row : row + 1, :], (SZ, PANEL))
            total = part_ref[start : start + SZ, :] + jnp.where(at_edge, term, 0.0)
            for o, refs, k in faces:
                for j in range(3):
                    at = slice(k * GROUP + j * SZ, k * GROUP + (j + 1) * SZ)
                    value = refs[0][at, :].astype(f32)
                    if len(refs) == 2:
                        value = jnp.where(low, value, refs[1][at, :].astype(f32))
                    total = total + lane(coef, o, i, j) * value
            stiff_ref[start : start + SZ, :] = total.astype(bf16)
    left_ref[...] = stiff_ref[...].T
    for t in range(modes_ref.shape[1] // PANEL):
        part = slice(t * PANEL, (t + 1) * PANEL)
        product = jnp.dot(left_ref[...], modes_ref[:, part], preferred_element_type=f32)
        low, high = product[:HALF], product[HALF:]
        keep = jnp.where(core == 0, low, high)
        send = jnp.where(core == 0, high, low).astype(bf16)
        for u in range(2):
            keep_ref[2 * t + u] = keep[:, u * HALF : (u + 1) * HALF]
            send_ref[2 * t + u] = send[:, u * HALF : (u + 1) * HALF]


def near_kernel(parts_ref, copies_ref):
    total = parts_ref[0].astype(f32)
    for k in range(1, parts_ref.shape[0]):
        total = total + parts_ref[k].astype(f32)
    total = total.astype(bf16)
    for k in range(copies_ref.shape[0]):
        copies_ref[k] = total


def fold_kernel(planes_ref, half_ref):
    for r in range(2):
        total = planes_ref[r].astype(f32)
        for q in range(1, 8):
            total = total + planes_ref[2 * q + r].astype(f32)
        half_ref[64 * r : 64 * (r + 1), :] = total


def flip_kernel(both_ref, out_ref):
    out_ref[...] = both_ref[...].T


def swap(value, axis):
    return lax.ppermute(value, axis, [(0, 1), (1, 0)])


def shards(modes, blocks, material):
    full = modes.shape[-1]
    flat = modes.transpose(0, 1, 3, 2, 4).reshape(ROWS, full)
    chain = [(i, i + 1) for i in range(15)]
    back = [(j, i) for i, j in chain]
    vmem = pl.BlockSpec(memory_space=pltpu.VMEM)
    shape = jax.ShapeDtypeStruct
    xside, yside = SY * GROUP, SX * GROUP
    panel, zsend, xinner, xouter, yfirst, ylast = pl.pallas_call(
        collect_kernel,
        in_specs=[pl.BlockSpec(memory_space=pl.ANY)],
        out_specs=[vmem] * 6,
        out_shape=[shape((2, ROWS, HALF), f32)]
        + [shape((rows, PANEL), bf16) for rows in (3 * CELLS, xside, xside, yside, yside)],
        scratch_shapes=[pltpu.VMEM((ROWS, PANEL), bf16), pltpu.VMEM((EDGE, PANEL), f32), pltpu.SemaphoreType.DMA],
        compiler_params=pltpu.CompilerParams(vmem_limit_bytes=50 << 20),
        name="collect_faces",
    )(flat)
    zface = swap(zsend, GZ)
    ylo = lax.ppermute(ylast, COL, chain)
    yhi = lax.ppermute(yfirst, COL, back)
    chip = swap(xinner, "core")
    pairs = [(i, i + 1) for i in range(1, 15, 2)]
    beside = lax.ppermute(xouter, ROW, pairs + [(j, i) for i, j in pairs])
    coef, part, near = pl.pallas_call(
        local_kernel,
        in_specs=[vmem] * 3 + [pl.BlockSpec(memory_space=pl.ANY)],
        out_specs=[vmem] * 3,
        out_shape=[shape((CELLS * SZ, 128), f32), shape((ROWS, PANEL), f32), shape((ROWS, full), bf16)],
        scratch_shapes=[
            pltpu.VMEM((NMAT, 128), f32),
            pltpu.VMEM((7, 4 * NMAT, 9 * HALF), bf16),
            pltpu.VMEM((5, CELLS * SZ, 4 * NMAT), bf16),
            pltpu.VMEM((7, CELLS * SZ, 9 * HALF), f32),
            pltpu.SemaphoreType.DMA,
        ],
        cost_estimate=pl.CostEstimate(flops=2 * ROWS * 21 * PANEL, bytes_accessed=3 * ROWS * PANEL, transcendentals=0),
        compiler_params=pltpu.CompilerParams(vmem_limit_bytes=46 << 20),
        name="local_stencil",
    )(material.transpose(1, 0, 2), blocks.transpose(2, 3, 0, 1), panel, flat)
    tiles = full // HALF
    term = pl.pallas_call(
        edge_kernel,
        in_specs=[vmem] * 2,
        out_specs=vmem,
        out_shape=shape((EDGE, PANEL), f32),
        cost_estimate=pl.CostEstimate(flops=4 * 10**9, bytes_accessed=EDGE * PANEL * 6, transcendentals=0),
        compiler_params=pltpu.CompilerParams(vmem_limit_bytes=8 << 20),
        name="edge_terms",
    )(zface, coef)
    keep, send = pl.pallas_call(
        product_kernel,
        in_specs=[vmem] * 8,
        out_specs=[vmem] * 2,
        out_shape=[shape((tiles, HALF, HALF), dtype) for dtype in (f32, bf16)],
        scratch_shapes=[pltpu.VMEM((ROWS, PANEL), bf16), pltpu.VMEM((PANEL, ROWS), bf16)],
        cost_estimate=pl.CostEstimate(flops=2 * ROWS * full * PANEL, bytes_accessed=2 * ROWS * full, transcendentals=0),
        compiler_params=pltpu.CompilerParams(vmem_limit_bytes=32 << 20),
        name="faces_and_product",
    )(ylo, yhi, chip, beside, coef, part, term, near)
    mine = (keep + swap(send, "core").astype(f32)).astype(bf16)
    parts = lax.all_to_all(mine.reshape(2 * tiles, HALF // 2, HALF), COL + ("zl",), 0, 0, tiled=True)
    copies = pl.pallas_call(
        near_kernel,
        in_specs=[vmem],
        out_specs=vmem,
        out_shape=shape((16, HALF // 2, HALF), bf16),
        compiler_params=pltpu.CompilerParams(vmem_limit_bytes=4 << 20),
        name="near_sum",
    )(parts)
    planes = lax.all_to_all(copies, Z, 0, 0, tiled=True)
    half = pl.pallas_call(
        fold_kernel,
        in_specs=[vmem],
        out_specs=vmem,
        out_shape=shape((HALF, HALF), f32),
        compiler_params=pltpu.CompilerParams(vmem_limit_bytes=4 << 20),
        name="fold",
    )(planes)
    both = lax.all_gather(half, "core", axis=0, tiled=True)
    return pl.pallas_call(
        flip_kernel,
        in_specs=[vmem],
        out_specs=vmem,
        out_shape=shape((HALF, PANEL), f32),
        compiler_params=pltpu.CompilerParams(vmem_limit_bytes=4 << 20),
        name="flip",
    )(both)


def solution(mesh):
    split = Mesh(mesh.devices.reshape(4, 2, 2, 4, 4, 2), ("zh", "zl", "core", "y", "x", "gz"))
    return jax.shard_map(
        shards,
        mesh=split,
        in_specs=(P(ROW, COL, GZ, None, None), P(), P(ROW, COL, GZ)),
        out_specs=P(COL, None),
        check_vma=False,
    )
```

```python
import jax
import jax.numpy as jnp
from jax import lax
from jax.experimental import pallas as pl
from jax.experimental.pallas import tpu as pltpu
from jax.sharding import Mesh, PartitionSpec as P

PANEL = 256
HALF = 128
NMAT = 8
SX, SY, SZ = 4, 6, 16
CELLS = SX * SY
GROUP = 3 * SZ
ROWS = CELLS * GROUP
EDGE = 3 * CELLS
ROW, COL, GZ = ("zh", "zl", "core"), ("y", "x"), "gz"
Z = ("gz", "zh", "zl")
f32, bf16 = jnp.float32, jnp.bfloat16


def lane(values, o, i, j, width=PANEL):
    k = (3 * i + j) * 7 + o
    return jnp.broadcast_to(values[:, k : k + 1], (values.shape[0], width))


def collect_kernel(modes_ref, panel_ref, z_ref, xin_ref, xout_ref, yin_ref, yout_ref, raw_ref, edge_ref, sem):
    copy = pltpu.make_async_copy(modes_ref.at[:, :PANEL], raw_ref, sem)
    copy.start()
    copy.wait()
    first = jnp.where(lax.axis_index(GZ) == 0, SZ - 1, 0)
    for h in range(2):
        part = slice(h * HALF, (h + 1) * HALF)
        panel_ref[h] = raw_ref[:, part].astype(f32)
        for j in range(3):
            rows = panel_ref.at[h][pl.ds(j * SZ + first, CELLS, stride=GROUP), :]
            edge_ref[j * CELLS : (j + 1) * CELLS, part] = rows
    z_ref[...] = edge_ref[...].astype(bf16)
    side = SY * GROUP
    low = lax.axis_index("core") == 0
    xin_ref[...] = jnp.where(low, raw_ref[ROWS - side :, :], raw_ref[:side, :])
    xout_ref[...] = jnp.where(low, raw_ref[:side, :], raw_ref[ROWS - side :, :])
    even = lax.axis_index("x") % 2 == 0
    for x in range(SX):
        near = raw_ref[x * side : x * side + GROUP, :]
        far = raw_ref[(x + 1) * side - GROUP : (x + 1) * side, :]
        yin_ref[x * GROUP : (x + 1) * GROUP, :] = jnp.where(even, far, near)
        yout_ref[x * GROUP : (x + 1) * GROUP, :] = jnp.where(even, near, far)


def split3(value):
    high = value.astype(bf16).astype(f32)
    mid = (value - high).astype(bf16).astype(f32)
    low = value - high - mid
    return jnp.concatenate([high, mid, low, jnp.zeros_like(value)]).astype(bf16)


def local_kernel(kind_ref, blocks_ref, panel_ref, modes_ref,
                 coef_ref, wall_ref, part_ref, near_ref, table_ref, wide_ref, hot_ref, plane_ref, sem):
    copy = pltpu.make_async_copy(modes_ref, near_ref, sem)
    copy.start()
    table_ref[...] = jnp.zeros((NMAT, 128), f32)
    for i in range(3):
        for j in range(3):
            k = 3 * i + j
            values = blocks_ref[i, j]
            table_ref[:, 7 * k : 7 * k + 7] = values
            for o in range(7):
                column = jnp.broadcast_to(values[:, o : o + 1], (NMAT, HALF))
                wide_ref[o, :, k * HALF : (k + 1) * HALF] = split3(column)
    kinds = jnp.concatenate([kind_ref[y] for y in range(SY)]).astype(f32).T
    slot = lax.broadcasted_iota(jnp.int32, (SZ, 4 * NMAT), 1)
    slot = jnp.where(slot < 3 * NMAT, slot % NMAT, -1).astype(f32)
    none = jnp.zeros((SZ, 4 * NMAT), bf16)
    for n in range(CELLS):
        x, y = divmod(n, SY)
        kind = jnp.broadcast_to(kinds[:, y * SX + x : y * SX + x + 1], (SZ, 4 * NMAT))
        hot = jnp.where(kind == slot, 1.0, 0.0).astype(bf16)
        outside = (False, x == SX - 1, x == 0, y == SY - 1, y == 0)
        for o in range(5):
            hot_ref[o, n * SZ : (n + 1) * SZ, :] = none if outside[o] else hot
    coef_ref[...] = jnp.dot(hot_ref[0], split3(table_ref[...]), preferred_element_type=f32)
    for o in range(7):
        plane_ref[o] = jnp.dot(hot_ref[o if o < 5 else 0], wide_ref[o], preferred_element_type=f32)
    whole = hot_ref[0]
    walls = (
        [(SX - 1) * SY + y for y in range(SY)],
        [y for y in range(SY)],
        [x * SY + SY - 1 for x in range(SX)],
        [x * SY for x in range(SX)],
    )
    for o, cells in enumerate(walls):
        rows = jnp.concatenate([whole[n * SZ : (n + 1) * SZ] for n in cells])
        wall_ref[o, : len(cells) * SZ, :] = jnp.dot(rows, wide_ref[o + 1], preferred_element_type=f32)
    level = lax.broadcasted_iota(jnp.int32, (SZ, HALF), 0)
    top, bottom = level == SZ - 1, level == 0

    def cell(n, carry):
        last = CELLS - 1
        sources = (
            (1, jnp.minimum(n + SY, last)),
            (2, jnp.maximum(n - SY, 0)),
            (3, jnp.minimum(n + 1, last)),
            (4, jnp.maximum(n - 1, 0)),
        )
        here = pl.ds(pl.multiple_of(n * SZ, SZ), SZ)
        total = [[jnp.zeros((SZ, HALF), f32) for _ in range(2)] for _ in range(3)]

        def rows(at, j):
            start = pl.multiple_of(at * GROUP + j * SZ, SZ)
            return [panel_ref[h, pl.ds(start, SZ), :] for h in range(2)]

        for j in range(3):
            own = rows(n, j)
            above = [jnp.where(top, 0.0, pltpu.roll(v, SZ - 1, 0)) for v in own]
            below = [jnp.where(bottom, 0.0, pltpu.roll(v, 1, 0)) for v in own]
            terms = [(0, own), (5, above), (6, below)] + [(o, rows(at, j)) for o, at in sources]
            for o, values in terms:
                for i in range(3):
                    k = 3 * i + j
                    factor = plane_ref[o, here, k * HALF : (k + 1) * HALF]
                    for h in range(2):
                        total[i][h] = total[i][h] + factor * values[h]
        for i in range(3):
            start = pl.multiple_of(n * GROUP + i * SZ, SZ)
            for h in range(2):
                part_ref[pl.ds(start, SZ), h * HALF : (h + 1) * HALF] = total[i][h]
        return carry

    lax.fori_loop(0, CELLS, cell, 0, unroll=2)
    copy.wait()


def edge_kernel(zface_ref, coef_ref, term_ref):
    gz = lax.axis_index(GZ)
    coef = coef_ref[pl.ds(jnp.where(gz == 0, SZ - 1, 0), CELLS, stride=SZ), :]
    coef = jnp.where(gz == 0, coef, pltpu.roll(coef, 127, 1))
    for i in range(3):
        total = jnp.zeros((CELLS, PANEL), f32)
        for j in range(3):
            total = total + lane(coef, 5, i, j) * zface_ref[j * CELLS : (j + 1) * CELLS, :].astype(f32)
        term_ref[i * CELLS : (i + 1) * CELLS, :] = total


def product_kernel(yin_ref, yout_ref, chip_ref, beside_ref, wall_ref, part_ref, term_ref, modes_ref,
                   keep_ref, send_ref, stiff_ref, left_ref):
    core, gz = lax.axis_index("core"), lax.axis_index(GZ)
    level = lax.broadcasted_iota(jnp.int32, (SZ, PANEL), 0)
    at_edge = level == jnp.where(gz == 0, SZ - 1, 0)
    low = core == 0
    even = lax.axis_index("x") % 2 == 0
    for n in range(CELLS):
        x, y = divmod(n, SY)
        faces = [(1, low, chip_ref, beside_ref, y)] if x == SX - 1 else []
        faces += [(2, low, beside_ref, chip_ref, y)] if x == 0 else []
        faces += [(3, even, yin_ref, yout_ref, x)] if y == SY - 1 else []
        faces += [(4, even, yout_ref, yin_ref, x)] if y == 0 else []
        for i in range(3):
            start = n * GROUP + i * SZ
            row = i * CELLS + n
            term = jnp.broadcast_to(term_ref[row : row + 1, :], (SZ, PANEL))
            total = part_ref[start : start + SZ, :] + jnp.where(at_edge, term, 0.0)
            for o, pick, one, two, cell in faces:
                for j in range(3):
                    at = slice(cell * GROUP + j * SZ, cell * GROUP + (j + 1) * SZ)
                    value = jnp.where(pick, one[at, :].astype(f32), two[at, :].astype(f32))
                    k = 3 * i + j
                    factor = wall_ref[o - 1, cell * SZ : (cell + 1) * SZ, k * HALF : (k + 1) * HALF]
                    total = total + jnp.concatenate([factor, factor], axis=1) * value
            stiff_ref[start : start + SZ, :] = total.astype(bf16)
    left_ref[...] = stiff_ref[...].T
    for t in range(modes_ref.shape[1] // PANEL):
        part = slice(t * PANEL, (t + 1) * PANEL)
        product = jnp.dot(left_ref[...], modes_ref[:, part], preferred_element_type=f32)
        low, high = product[:HALF], product[HALF:]
        keep = jnp.where(core == 0, low, high)
        send = jnp.where(core == 0, high, low).astype(bf16)
        for u in range(2):
            keep_ref[2 * t + u] = keep[:, u * HALF : (u + 1) * HALF]
            send_ref[2 * t + u] = send[:, u * HALF : (u + 1) * HALF]


def near_kernel(parts_ref, copies_ref):
    total = parts_ref[0].astype(f32)
    for k in range(1, parts_ref.shape[0]):
        total = total + parts_ref[k].astype(f32)
    total = total.astype(bf16)
    for k in range(copies_ref.shape[0]):
        copies_ref[k] = total


def fold_kernel(planes_ref, half_ref):
    for r in range(2):
        total = planes_ref[r].astype(f32)
        for q in range(1, 8):
            total = total + planes_ref[2 * q + r].astype(f32)
        half_ref[64 * r : 64 * (r + 1), :] = total


def flip_kernel(both_ref, out_ref):
    out_ref[...] = both_ref[...].T


def swap(value, axis):
    return lax.ppermute(value, axis, [(0, 1), (1, 0)])


def shards(modes, blocks, material):
    full = modes.shape[-1]
    flat = modes.transpose(0, 1, 3, 2, 4).reshape(ROWS, full)
    vmem = pl.BlockSpec(memory_space=pltpu.VMEM)
    shape = jax.ShapeDtypeStruct
    xside, yside = SY * GROUP, SX * GROUP
    panel, zsend, xinner, xouter, yinner, youter = pl.pallas_call(
        collect_kernel,
        in_specs=[pl.BlockSpec(memory_space=pl.ANY)],
        out_specs=[vmem] * 6,
        out_shape=[shape((2, ROWS, HALF), f32)]
        + [shape((rows, PANEL), bf16) for rows in (3 * CELLS, xside, xside, yside, yside)],
        scratch_shapes=[pltpu.VMEM((ROWS, PANEL), bf16), pltpu.VMEM((EDGE, PANEL), f32), pltpu.SemaphoreType.DMA],
        compiler_params=pltpu.CompilerParams(vmem_limit_bytes=50 << 20),
        name="collect_faces",
    )(flat)
    zface = swap(zsend, GZ)

    def pairs(start):
        ends = [(i, i + 1) for i in range(start, 15, 2)]
        return ends + [(j, i) for i, j in ends]

    yin = lax.ppermute(yinner, COL, pairs(0))
    yout = lax.ppermute(youter, COL, pairs(1))
    chip = swap(xinner, "core")
    beside = lax.ppermute(xouter, ROW, pairs(1))
    coef, wall, part, near = pl.pallas_call(
        local_kernel,
        in_specs=[vmem] * 3 + [pl.BlockSpec(memory_space=pl.ANY)],
        out_specs=[vmem] * 4,
        out_shape=[shape((CELLS * SZ, 128), f32), shape((4, SY * SZ, 9 * HALF), f32), shape((ROWS, PANEL), f32), shape((ROWS, full), bf16)],
        scratch_shapes=[
            pltpu.VMEM((NMAT, 128), f32),
            pltpu.VMEM((7, 4 * NMAT, 9 * HALF), bf16),
            pltpu.VMEM((5, CELLS * SZ, 4 * NMAT), bf16),
            pltpu.VMEM((7, CELLS * SZ, 9 * HALF), f32),
            pltpu.SemaphoreType.DMA,
        ],
        cost_estimate=pl.CostEstimate(flops=2 * ROWS * 21 * PANEL, bytes_accessed=3 * ROWS * PANEL, transcendentals=0),
        compiler_params=pltpu.CompilerParams(vmem_limit_bytes=44 << 20),
        name="local_stencil",
    )(material.transpose(1, 0, 2), blocks.transpose(2, 3, 0, 1), panel, flat)
    tiles = full // HALF
    term = pl.pallas_call(
        edge_kernel,
        in_specs=[vmem] * 2,
        out_specs=vmem,
        out_shape=shape((EDGE, PANEL), f32),
        cost_estimate=pl.CostEstimate(flops=4 * 10**9, bytes_accessed=EDGE * PANEL * 6, transcendentals=0),
        compiler_params=pltpu.CompilerParams(vmem_limit_bytes=8 << 20),
        name="edge_terms",
    )(zface, coef)
    keep, send = pl.pallas_call(
        product_kernel,
        in_specs=[vmem] * 8,
        out_specs=[vmem] * 2,
        out_shape=[shape((tiles, HALF, HALF), dtype) for dtype in (f32, bf16)],
        scratch_shapes=[pltpu.VMEM((ROWS, PANEL), bf16), pltpu.VMEM((PANEL, ROWS), bf16)],
        cost_estimate=pl.CostEstimate(flops=2 * ROWS * full * PANEL, bytes_accessed=2 * ROWS * full, transcendentals=0),
        compiler_params=pltpu.CompilerParams(vmem_limit_bytes=32 << 20),
        name="faces_and_product",
    )(yin, yout, chip, beside, wall, part, term, near)
    mine = (keep + swap(send, "core").astype(f32)).astype(bf16)
    parts = lax.all_to_all(mine.reshape(2 * tiles, HALF // 2, HALF), COL + ("zl",), 0, 0, tiled=True)
    copies = pl.pallas_call(
        near_kernel,
        in_specs=[vmem],
        out_specs=vmem,
        out_shape=shape((16, HALF // 2, HALF), bf16),
        compiler_params=pltpu.CompilerParams(vmem_limit_bytes=4 << 20),
        name="near_sum",
    )(parts)
    planes = lax.all_to_all(copies, Z, 0, 0, tiled=True)
    half = pl.pallas_call(
        fold_kernel,
        in_specs=[vmem],
        out_specs=vmem,
        out_shape=shape((HALF, HALF), f32),
        compiler_params=pltpu.CompilerParams(vmem_limit_bytes=4 << 20),
        name="fold",
    )(planes)
    both = lax.all_gather(half, "core", axis=0, tiled=True)
    return pl.pallas_call(
        flip_kernel,
        in_specs=[vmem],
        out_specs=vmem,
        out_shape=shape((HALF, PANEL), f32),
        compiler_params=pltpu.CompilerParams(vmem_limit_bytes=4 << 20),
        name="flip",
    )(both)


def solution(mesh):
    split = Mesh(mesh.devices.reshape(4, 2, 2, 4, 4, 2), ("zh", "zl", "core", "y", "x", "gz"))
    return jax.shard_map(
        shards,
        mesh=split,
        in_specs=(P(ROW, COL, GZ, None, None), P(), P(ROW, COL, GZ)),
        out_specs=P(COL, None),
        check_vma=False,
    )
```

```python
import jax
import jax.numpy as jnp
from jax import lax
from jax.experimental import pallas as pl
from jax.experimental.pallas import tpu as pltpu
from jax.sharding import Mesh, PartitionSpec as P

PANEL = 256
HALF = 128
NMAT = 8
SX, SY, SZ = 4, 6, 16
CELLS = SX * SY
GROUP = 3 * SZ
ROWS = CELLS * GROUP
EDGE = 3 * CELLS
ROW, COL, GZ = ("zh", "zl", "core"), ("y", "x"), "gz"
Z = ("gz", "zh", "zl")
f32, bf16 = jnp.float32, jnp.bfloat16


def lane(values, o, i, j, width=PANEL):
    k = (3 * i + j) * 7 + o
    return jnp.broadcast_to(values[:, k : k + 1], (values.shape[0], width))


def collect_kernel(modes_ref, panel_ref, z_ref, xin_ref, xout_ref, yin_ref, yout_ref, raw_ref, edge_ref, sem):
    copy = pltpu.make_async_copy(modes_ref.at[:, :PANEL], raw_ref, sem)
    copy.start()
    copy.wait()
    first = jnp.where(lax.axis_index(GZ) == 0, SZ - 1, 0)
    for h in range(2):
        part = slice(h * HALF, (h + 1) * HALF)
        panel_ref[h] = raw_ref[:, part].astype(f32)
        for j in range(3):
            rows = panel_ref.at[h][pl.ds(j * SZ + first, CELLS, stride=GROUP), :]
            edge_ref[j * CELLS : (j + 1) * CELLS, part] = rows
    z_ref[...] = edge_ref[...].astype(bf16)
    side = SY * GROUP
    low = lax.axis_index("core") == 0
    xin_ref[...] = jnp.where(low, raw_ref[ROWS - side :, :], raw_ref[:side, :])
    xout_ref[...] = jnp.where(low, raw_ref[:side, :], raw_ref[ROWS - side :, :])
    even = lax.axis_index("x") % 2 == 0
    for x in range(SX):
        near = raw_ref[x * side : x * side + GROUP, :]
        far = raw_ref[(x + 1) * side - GROUP : (x + 1) * side, :]
        yin_ref[x * GROUP : (x + 1) * GROUP, :] = jnp.where(even, far, near)
        yout_ref[x * GROUP : (x + 1) * GROUP, :] = jnp.where(even, near, far)


def split3(value):
    high = value.astype(bf16).astype(f32)
    mid = (value - high).astype(bf16).astype(f32)
    low = value - high - mid
    return jnp.concatenate([high, mid, low, jnp.zeros_like(value)]).astype(bf16)


def local_kernel(kind_ref, blocks_ref, panel_ref, modes_ref,
                 coef_ref, wall_ref, part_ref, near_ref, table_ref, wide_ref, hot_ref, plane_ref, sem):
    copy = pltpu.make_async_copy(modes_ref, near_ref, sem)
    copy.start()
    table_ref[...] = jnp.zeros((NMAT, 128), f32)
    for i in range(3):
        for j in range(3):
            k = 3 * i + j
            values = blocks_ref[i, j]
            table_ref[:, 7 * k : 7 * k + 7] = values
            for o in range(7):
                column = jnp.broadcast_to(values[:, o : o + 1], (NMAT, HALF))
                wide_ref[o, :, k * HALF : (k + 1) * HALF] = split3(column)
    kinds = jnp.concatenate([kind_ref[y] for y in range(SY)]).astype(f32).T
    slot = lax.broadcasted_iota(jnp.int32, (SZ, 4 * NMAT), 1)
    slot = jnp.where(slot < 3 * NMAT, slot % NMAT, -1).astype(f32)
    none = jnp.zeros((SZ, 4 * NMAT), bf16)
    for n in range(CELLS):
        x, y = divmod(n, SY)
        kind = jnp.broadcast_to(kinds[:, y * SX + x : y * SX + x + 1], (SZ, 4 * NMAT))
        hot = jnp.where(kind == slot, 1.0, 0.0).astype(bf16)
        outside = (False, x == SX - 1, x == 0, y == SY - 1, y == 0)
        for o in range(5):
            hot_ref[o, n * SZ : (n + 1) * SZ, :] = none if outside[o] else hot
    coef_ref[...] = jnp.dot(hot_ref[0], split3(table_ref[...]), preferred_element_type=f32)
    for o in range(7):
        plane_ref[o] = jnp.dot(hot_ref[o if o < 5 else 0], wide_ref[o], preferred_element_type=f32)
    whole = hot_ref[0]
    walls = (
        [(SX - 1) * SY + y for y in range(SY)],
        [y for y in range(SY)],
        [x * SY + SY - 1 for x in range(SX)],
        [x * SY for x in range(SX)],
    )
    for o, cells in enumerate(walls):
        rows = jnp.concatenate([whole[n * SZ : (n + 1) * SZ] for n in cells])
        wall_ref[o, : len(cells) * SZ, :] = jnp.dot(rows, wide_ref[o + 1], preferred_element_type=f32)
    level = lax.broadcasted_iota(jnp.int32, (SZ, HALF), 0)
    top, bottom = level == SZ - 1, level == 0

    def cell(n, carry):
        last = CELLS - 1
        sources = (
            (1, jnp.minimum(n + SY, last)),
            (2, jnp.maximum(n - SY, 0)),
            (3, jnp.minimum(n + 1, last)),
            (4, jnp.maximum(n - 1, 0)),
        )
        here = pl.ds(pl.multiple_of(n * SZ, SZ), SZ)
        total = [[jnp.zeros((SZ, HALF), f32) for _ in range(2)] for _ in range(3)]

        def rows(at, j):
            start = pl.multiple_of(at * GROUP + j * SZ, SZ)
            return [panel_ref[h, pl.ds(start, SZ), :] for h in range(2)]

        for j in range(3):
            own = rows(n, j)
            above = [jnp.where(top, 0.0, pltpu.roll(v, SZ - 1, 0)) for v in own]
            below = [jnp.where(bottom, 0.0, pltpu.roll(v, 1, 0)) for v in own]
            terms = [(0, own), (5, above), (6, below)] + [(o, rows(at, j)) for o, at in sources]
            for o, values in terms:
                for i in range(3):
                    k = 3 * i + j
                    factor = plane_ref[o, here, k * HALF : (k + 1) * HALF]
                    for h in range(2):
                        total[i][h] = total[i][h] + factor * values[h]
        for i in range(3):
            start = pl.multiple_of(n * GROUP + i * SZ, SZ)
            for h in range(2):
                part_ref[pl.ds(start, SZ), h * HALF : (h + 1) * HALF] = total[i][h]
        return carry

    lax.fori_loop(0, CELLS, cell, 0, unroll=2)
    copy.wait()


def edge_kernel(zface_ref, coef_ref, term_ref):
    gz = lax.axis_index(GZ)
    coef = coef_ref[pl.ds(jnp.where(gz == 0, SZ - 1, 0), CELLS, stride=SZ), :]
    coef = jnp.where(gz == 0, coef, pltpu.roll(coef, 127, 1))
    for i in range(3):
        total = jnp.zeros((CELLS, PANEL), f32)
        for j in range(3):
            total = total + lane(coef, 5, i, j) * zface_ref[j * CELLS : (j + 1) * CELLS, :].astype(f32)
        term_ref[i * CELLS : (i + 1) * CELLS, :] = total


def product_kernel(yin_ref, yout_ref, chip_ref, beside_ref, wall_ref, part_ref, term_ref, modes_ref,
                   keep_ref, send_ref, stiff_ref, left_ref):
    core, gz = lax.axis_index("core"), lax.axis_index(GZ)
    level = lax.broadcasted_iota(jnp.int32, (SZ, PANEL), 0)
    at_edge = level == jnp.where(gz == 0, SZ - 1, 0)
    low = core == 0
    even = lax.axis_index("x") % 2 == 0
    for n in range(CELLS):
        x, y = divmod(n, SY)
        faces = [(1, low, chip_ref, beside_ref, y)] if x == SX - 1 else []
        faces += [(2, low, beside_ref, chip_ref, y)] if x == 0 else []
        faces += [(3, even, yin_ref, yout_ref, x)] if y == SY - 1 else []
        faces += [(4, even, yout_ref, yin_ref, x)] if y == 0 else []
        for i in range(3):
            start = n * GROUP + i * SZ
            row = i * CELLS + n
            term = jnp.broadcast_to(term_ref[row : row + 1, :], (SZ, PANEL))
            total = part_ref[start : start + SZ, :] + jnp.where(at_edge, term, 0.0)
            for o, pick, one, two, cell in faces:
                for j in range(3):
                    at = slice(cell * GROUP + j * SZ, cell * GROUP + (j + 1) * SZ)
                    value = jnp.where(pick, one[at, :].astype(f32), two[at, :].astype(f32))
                    k = 3 * i + j
                    factor = wall_ref[o - 1, cell * SZ : (cell + 1) * SZ, k * HALF : (k + 1) * HALF]
                    total = total + jnp.concatenate([factor, factor], axis=1) * value
            stiff_ref[start : start + SZ, :] = total.astype(bf16)
    left_ref[...] = stiff_ref[...].T
    for t in range(modes_ref.shape[1] // PANEL):
        part = slice(t * PANEL, (t + 1) * PANEL)
        product = jnp.dot(left_ref[...], modes_ref[:, part], preferred_element_type=f32)
        low, high = product[:HALF], product[HALF:]
        keep = jnp.where(core == 0, low, high)
        send = jnp.where(core == 0, high, low).astype(bf16)
        for u in range(2):
            keep_ref[2 * t + u] = keep[:, u * HALF : (u + 1) * HALF]
            send_ref[2 * t + u] = send[:, u * HALF : (u + 1) * HALF]


def near_kernel(parts_ref, copies_ref):
    total = parts_ref[0].astype(f32)
    for k in range(1, parts_ref.shape[0]):
        total = total + parts_ref[k].astype(f32)
    total = total.astype(bf16)
    for k in range(copies_ref.shape[0]):
        copies_ref[k] = total


def fold_kernel(planes_ref, half_ref):
    for r in range(2):
        total = planes_ref[r].astype(f32)
        for q in range(1, 8):
            total = total + planes_ref[2 * q + r].astype(f32)
        half_ref[64 * r : 64 * (r + 1), :] = total


def flip_kernel(both_ref, out_ref):
    out_ref[...] = both_ref[...].T


def swap(value, axis):
    return lax.ppermute(value, axis, [(0, 1), (1, 0)])


def shards(modes, blocks, material):
    full = modes.shape[-1]
    flat = modes.transpose(0, 1, 3, 2, 4).reshape(ROWS, full)
    vmem = pl.BlockSpec(memory_space=pltpu.VMEM)
    shape = jax.ShapeDtypeStruct
    xside, yside = SY * GROUP, SX * GROUP
    panel, zsend, xinner, xouter, yinner, youter = pl.pallas_call(
        collect_kernel,
        in_specs=[pl.BlockSpec(memory_space=pl.ANY)],
        out_specs=[vmem] * 6,
        out_shape=[shape((2, ROWS, HALF), f32)]
        + [shape((rows, PANEL), bf16) for rows in (3 * CELLS, xside, xside, yside, yside)],
        scratch_shapes=[pltpu.VMEM((ROWS, PANEL), bf16), pltpu.VMEM((EDGE, PANEL), f32), pltpu.SemaphoreType.DMA],
        compiler_params=pltpu.CompilerParams(vmem_limit_bytes=50 << 20),
        name="collect_faces",
    )(flat)
    zface = swap(zsend, GZ)

    def pairs(start):
        ends = [(i, i + 1) for i in range(start, 15, 2)]
        return ends + [(j, i) for i, j in ends]

    yin = lax.ppermute(yinner, COL, pairs(0))
    yout = lax.ppermute(youter, COL, pairs(1))
    chip = swap(xinner, "core")
    beside = lax.ppermute(xouter, ROW, pairs(1))
    coef, wall, part, near = pl.pallas_call(
        local_kernel,
        in_specs=[vmem] * 3 + [pl.BlockSpec(memory_space=pl.ANY)],
        out_specs=[vmem] * 4,
        out_shape=[shape((CELLS * SZ, 128), f32), shape((4, SY * SZ, 9 * HALF), f32), shape((ROWS, PANEL), f32), shape((ROWS, full), bf16)],
        scratch_shapes=[
            pltpu.VMEM((NMAT, 128), f32),
            pltpu.VMEM((7, 4 * NMAT, 9 * HALF), bf16),
            pltpu.VMEM((5, CELLS * SZ, 4 * NMAT), bf16),
            pltpu.VMEM((7, CELLS * SZ, 9 * HALF), f32),
            pltpu.SemaphoreType.DMA,
        ],
        cost_estimate=pl.CostEstimate(flops=2 * ROWS * 21 * PANEL, bytes_accessed=3 * ROWS * PANEL, transcendentals=0),
        compiler_params=pltpu.CompilerParams(vmem_limit_bytes=44 << 20),
        name="local_stencil",
    )(material.transpose(1, 0, 2), blocks.transpose(2, 3, 0, 1), panel, flat)
    tiles = full // HALF
    term = pl.pallas_call(
        edge_kernel,
        in_specs=[vmem] * 2,
        out_specs=vmem,
        out_shape=shape((EDGE, PANEL), f32),
        cost_estimate=pl.CostEstimate(flops=95 * 10**7, bytes_accessed=EDGE * PANEL * 6, transcendentals=0),
        compiler_params=pltpu.CompilerParams(vmem_limit_bytes=8 << 20),
        name="edge_terms",
    )(zface, coef)
    keep, send = pl.pallas_call(
        product_kernel,
        in_specs=[vmem] * 8,
        out_specs=[vmem] * 2,
        out_shape=[shape((tiles, HALF, HALF), dtype) for dtype in (f32, bf16)],
        scratch_shapes=[pltpu.VMEM((ROWS, PANEL), bf16), pltpu.VMEM((PANEL, ROWS), bf16)],
        cost_estimate=pl.CostEstimate(flops=2 * ROWS * full * PANEL, bytes_accessed=2 * ROWS * full, transcendentals=0),
        compiler_params=pltpu.CompilerParams(vmem_limit_bytes=32 << 20),
        name="faces_and_product",
    )(yin, yout, chip, beside, wall, part, term, near)
    mine = (keep + swap(send, "core").astype(f32)).astype(bf16)
    parts = lax.all_to_all(mine.reshape(2 * tiles, HALF // 2, HALF), COL + ("zl",), 0, 0, tiled=True)
    copies = pl.pallas_call(
        near_kernel,
        in_specs=[vmem],
        out_specs=vmem,
        out_shape=shape((16, HALF // 2, HALF), bf16),
        compiler_params=pltpu.CompilerParams(vmem_limit_bytes=4 << 20),
        name="near_sum",
    )(parts)
    planes = lax.all_to_all(copies, Z, 0, 0, tiled=True)
    half = pl.pallas_call(
        fold_kernel,
        in_specs=[vmem],
        out_specs=vmem,
        out_shape=shape((HALF, HALF), f32),
        compiler_params=pltpu.CompilerParams(vmem_limit_bytes=4 << 20),
        name="fold",
    )(planes)
    both = lax.all_gather(half, "core", axis=0, tiled=True)
    return pl.pallas_call(
        flip_kernel,
        in_specs=[vmem],
        out_specs=vmem,
        out_shape=shape((HALF, PANEL), f32),
        compiler_params=pltpu.CompilerParams(vmem_limit_bytes=4 << 20),
        name="flip",
    )(both)


def solution(mesh):
    split = Mesh(mesh.devices.reshape(4, 2, 2, 4, 4, 2), ("zh", "zl", "core", "y", "x", "gz"))
    return jax.shard_map(
        shards,
        mesh=split,
        in_specs=(P(ROW, COL, GZ, None, None), P(), P(ROW, COL, GZ)),
        out_specs=P(COL, None),
        check_vma=False,
    )
```

```python
import jax
import jax.numpy as jnp
from jax import lax
from jax.experimental import pallas as pl
from jax.experimental.pallas import tpu as pltpu
from jax.sharding import Mesh, PartitionSpec as P

PANEL = 256
HALF = 128
NMAT = 8
SX, SY, SZ = 4, 6, 16
CELLS = SX * SY
GROUP = 3 * SZ
ROWS = CELLS * GROUP
EDGE = 3 * CELLS
ROW, COL, GZ = ("zh", "zl", "core"), ("y", "x"), "gz"
Z = ("gz", "zh", "zl")
f32, bf16 = jnp.float32, jnp.bfloat16


def lane(values, o, i, j, width=PANEL):
    k = (3 * i + j) * 7 + o
    return jnp.broadcast_to(values[:, k : k + 1], (values.shape[0], width))


def collect_kernel(modes_ref, panel_ref, z_ref, xin_ref, xout_ref, yin_ref, yout_ref, raw_ref, edge_ref, sem):
    copy = pltpu.make_async_copy(modes_ref.at[:, :PANEL], raw_ref, sem)
    copy.start()
    copy.wait()
    first = jnp.where(lax.axis_index(GZ) == 0, SZ - 1, 0)
    for h in range(2):
        part = slice(h * HALF, (h + 1) * HALF)
        panel_ref[h] = raw_ref[:, part].astype(f32)
        for j in range(3):
            rows = panel_ref.at[h][pl.ds(j * SZ + first, CELLS, stride=GROUP), :]
            edge_ref[j * CELLS : (j + 1) * CELLS, part] = rows
    z_ref[...] = edge_ref[...].astype(bf16)
    side = SY * GROUP
    low = lax.axis_index("core") == 0
    xin_ref[...] = jnp.where(low, raw_ref[ROWS - side :, :], raw_ref[:side, :])
    xout_ref[...] = jnp.where(low, raw_ref[:side, :], raw_ref[ROWS - side :, :])
    even = lax.axis_index("x") % 2 == 0
    for x in range(SX):
        near = raw_ref[x * side : x * side + GROUP, :]
        far = raw_ref[(x + 1) * side - GROUP : (x + 1) * side, :]
        yin_ref[x * GROUP : (x + 1) * GROUP, :] = jnp.where(even, far, near)
        yout_ref[x * GROUP : (x + 1) * GROUP, :] = jnp.where(even, near, far)


def split3(value):
    high = value.astype(bf16).astype(f32)
    mid = (value - high).astype(bf16).astype(f32)
    return high, mid, value - high - mid


def stack3(value):
    return jnp.concatenate([*split3(value), jnp.zeros_like(value)]).astype(bf16)


def local_kernel(kind_ref, blocks_ref, panel_ref, modes_ref,
                 coef_ref, wall_ref, part_ref, near_ref,
                 table_ref, wide_ref, hot_ref, text_ref, weight_ref, place_ref, matrix_ref, grid_ref, sem):
    copy = pltpu.make_async_copy(modes_ref, near_ref, sem)
    copy.start()
    table_ref[...] = jnp.zeros((NMAT, 128), f32)
    text_ref[...] = jnp.zeros(text_ref.shape, f32)
    for i in range(3):
        for j in range(3):
            k = 3 * i + j
            values = blocks_ref[i, j]
            table_ref[:, 7 * k : 7 * k + 7] = values
            for o in range(7):
                column = jnp.broadcast_to(values[:, o : o + 1], (NMAT, HALF))
                own, at = (0, o * GROUP) if o < 5 else (o - 4, 0)
                at += j * SZ
                text_ref[own, i, :, at : at + SZ] = column[:, :SZ]
                if 1 <= o <= 4:
                    wide_ref[o - 1, :, k * HALF : (k + 1) * HALF] = stack3(column)
    row = lax.broadcasted_iota(jnp.int32, (SZ, PANEL), 0)
    column = lax.broadcasted_iota(jnp.int32, (SZ, PANEL), 1)
    same = column % SZ == row
    above = (column % SZ == row + 1) & (column < GROUP)
    below = (column % SZ == row - 1) & (column < GROUP)
    for i in range(3):
        for m in range(NMAT):
            here, up, down = [jnp.broadcast_to(text_ref[own, i, m : m + 1, :], (SZ, PANEL)) for own in range(3)]
            value = jnp.where(same, here, jnp.where(above, up, jnp.where(below, down, 0.0)))
            for part, piece in enumerate(split3(value)):
                weight_ref[part, i, m * SZ : (m + 1) * SZ, :] = piece.astype(bf16)
    kinds = jnp.concatenate([kind_ref[y] for y in range(SY)]).astype(f32).T
    slot = lax.broadcasted_iota(jnp.int32, (SZ, 4 * NMAT), 1)
    slot = jnp.where(slot < 3 * NMAT, slot % NMAT, -1).astype(f32)
    spot = column[:, :128]
    spot = jnp.where(spot % SZ == row[:, :128], spot // SZ, -1).astype(f32)
    none = jnp.zeros((GROUP, PANEL), bf16)
    for n in range(CELLS):
        x, y = divmod(n, SY)
        kind = jnp.broadcast_to(kinds[:, y * SX + x : y * SX + x + 1], (SZ, 128))
        here = slice(n * SZ, (n + 1) * SZ)
        hot_ref[here, :] = jnp.where(kind[:, : 4 * NMAT] == slot, 1.0, 0.0).astype(bf16)
        place_ref[here, :] = jnp.where(kind == spot, 1.0, 0.0).astype(bf16)
        rows = [panel_ref[h, n * GROUP : (n + 1) * GROUP, :] for h in range(2)]
        grid_ref[(x + 1) * (SY + 2) + y + 1] = jnp.concatenate(rows, axis=1).astype(bf16)
    for y in range(SY + 2):
        grid_ref[y] = none
        grid_ref[(SX + 1) * (SY + 2) + y] = none
    for x in range(1, SX + 1):
        grid_ref[x * (SY + 2)] = none
        grid_ref[x * (SY + 2) + SY + 1] = none
    coef_ref[...] = jnp.dot(hot_ref[...], stack3(table_ref[...]), preferred_element_type=f32)
    walls = (
        [(SX - 1) * SY + y for y in range(SY)],
        [y for y in range(SY)],
        [x * SY + SY - 1 for x in range(SX)],
        [x * SY for x in range(SX)],
    )
    for o, cells in enumerate(walls):
        rows = jnp.concatenate([hot_ref[n * SZ : (n + 1) * SZ, :] for n in cells])
        wall_ref[o, : len(cells) * SZ, :] = jnp.dot(rows, wide_ref[o], preferred_element_type=f32)
    for i in range(3):
        for part in range(3):
            product = jnp.dot(place_ref[...], weight_ref[part, i], preferred_element_type=f32)
            matrix_ref[part, i] = product.astype(bf16)
    pad = jnp.zeros((SZ, PANEL), bf16)
    for n in range(CELLS):
        at = (n // SY + 1) * (SY + 2) + n % SY + 1
        here = slice(n * SZ, (n + 1) * SZ)
        left = jnp.concatenate([matrix_ref[part, i, here, :] for part in range(3) for i in range(3)])
        right = jnp.concatenate([grid_ref[k] for k in (at, at + SY + 2, at - SY - 2, at + 1, at - 1)] + [pad])
        out = jnp.dot(left, right, preferred_element_type=f32)
        part_ref[n * GROUP : (n + 1) * GROUP, :] = (out[2 * GROUP :] + out[GROUP : 2 * GROUP]) + out[:GROUP]
    copy.wait()


def edge_kernel(zface_ref, coef_ref, term_ref):
    gz = lax.axis_index(GZ)
    coef = coef_ref[pl.ds(jnp.where(gz == 0, SZ - 1, 0), CELLS, stride=SZ), :]
    coef = jnp.where(gz == 0, coef, pltpu.roll(coef, 127, 1))
    for i in range(3):
        total = jnp.zeros((CELLS, PANEL), f32)
        for j in range(3):
            total = total + lane(coef, 5, i, j) * zface_ref[j * CELLS : (j + 1) * CELLS, :].astype(f32)
        term_ref[i * CELLS : (i + 1) * CELLS, :] = total


def product_kernel(yin_ref, yout_ref, chip_ref, beside_ref, wall_ref, part_ref, term_ref, modes_ref,
                   keep_ref, send_ref, stiff_ref, left_ref):
    core, gz = lax.axis_index("core"), lax.axis_index(GZ)
    level = lax.broadcasted_iota(jnp.int32, (SZ, PANEL), 0)
    at_edge = level == jnp.where(gz == 0, SZ - 1, 0)
    low = core == 0
    even = lax.axis_index("x") % 2 == 0
    for n in range(CELLS):
        x, y = divmod(n, SY)
        faces = [(1, low, chip_ref, beside_ref, y)] if x == SX - 1 else []
        faces += [(2, low, beside_ref, chip_ref, y)] if x == 0 else []
        faces += [(3, even, yin_ref, yout_ref, x)] if y == SY - 1 else []
        faces += [(4, even, yout_ref, yin_ref, x)] if y == 0 else []
        for i in range(3):
            start = n * GROUP + i * SZ
            row = i * CELLS + n
            term = jnp.broadcast_to(term_ref[row : row + 1, :], (SZ, PANEL))
            total = part_ref[start : start + SZ, :] + jnp.where(at_edge, term, 0.0)
            for o, pick, one, two, cell in faces:
                for j in range(3):
                    at = slice(cell * GROUP + j * SZ, cell * GROUP + (j + 1) * SZ)
                    value = jnp.where(pick, one[at, :].astype(f32), two[at, :].astype(f32))
                    k = 3 * i + j
                    factor = wall_ref[o - 1, cell * SZ : (cell + 1) * SZ, k * HALF : (k + 1) * HALF]
                    total = total + jnp.concatenate([factor, factor], axis=1) * value
            stiff_ref[start : start + SZ, :] = total.astype(bf16)
    left_ref[...] = stiff_ref[...].T
    for t in range(modes_ref.shape[1] // PANEL):
        part = slice(t * PANEL, (t + 1) * PANEL)
        product = jnp.dot(left_ref[...], modes_ref[:, part], preferred_element_type=f32)
        low, high = product[:HALF], product[HALF:]
        keep = jnp.where(core == 0, low, high)
        send = jnp.where(core == 0, high, low).astype(bf16)
        for u in range(2):
            keep_ref[2 * t + u] = keep[:, u * HALF : (u + 1) * HALF]
            send_ref[2 * t + u] = send[:, u * HALF : (u + 1) * HALF]


def near_kernel(parts_ref, copies_ref):
    total = parts_ref[0].astype(f32)
    for k in range(1, parts_ref.shape[0]):
        total = total + parts_ref[k].astype(f32)
    total = total.astype(bf16)
    for k in range(copies_ref.shape[0]):
        copies_ref[k] = total


def fold_kernel(planes_ref, half_ref):
    for r in range(2):
        total = planes_ref[r].astype(f32)
        for q in range(1, 8):
            total = total + planes_ref[2 * q + r].astype(f32)
        half_ref[64 * r : 64 * (r + 1), :] = total


def flip_kernel(both_ref, out_ref):
    out_ref[...] = both_ref[...].T


def swap(value, axis):
    return lax.ppermute(value, axis, [(0, 1), (1, 0)])


def shards(modes, blocks, material):
    full = modes.shape[-1]
    flat = modes.transpose(0, 1, 3, 2, 4).reshape(ROWS, full)
    vmem = pl.BlockSpec(memory_space=pltpu.VMEM)
    shape = jax.ShapeDtypeStruct
    xside, yside = SY * GROUP, SX * GROUP
    panel, zsend, xinner, xouter, yinner, youter = pl.pallas_call(
        collect_kernel,
        in_specs=[pl.BlockSpec(memory_space=pl.ANY)],
        out_specs=[vmem] * 6,
        out_shape=[shape((2, ROWS, HALF), f32)]
        + [shape((rows, PANEL), bf16) for rows in (3 * CELLS, xside, xside, yside, yside)],
        scratch_shapes=[pltpu.VMEM((ROWS, PANEL), bf16), pltpu.VMEM((EDGE, PANEL), f32), pltpu.SemaphoreType.DMA],
        compiler_params=pltpu.CompilerParams(vmem_limit_bytes=50 << 20),
        name="collect_faces",
    )(flat)
    zface = swap(zsend, GZ)

    def pairs(start):
        ends = [(i, i + 1) for i in range(start, 15, 2)]
        return ends + [(j, i) for i, j in ends]

    yin = lax.ppermute(yinner, COL, pairs(0))
    yout = lax.ppermute(youter, COL, pairs(1))
    chip = swap(xinner, "core")
    beside = lax.ppermute(xouter, ROW, pairs(1))
    coef, wall, part, near = pl.pallas_call(
        local_kernel,
        in_specs=[vmem] * 3 + [pl.BlockSpec(memory_space=pl.ANY)],
        out_specs=[vmem] * 4,
        out_shape=[shape((CELLS * SZ, 128), f32), shape((4, SY * SZ, 9 * HALF), f32), shape((ROWS, PANEL), f32), shape((ROWS, full), bf16)],
        scratch_shapes=[
            pltpu.VMEM((NMAT, 128), f32),
            pltpu.VMEM((4, 4 * NMAT, 9 * HALF), bf16),
            pltpu.VMEM((CELLS * SZ, 4 * NMAT), bf16),
            pltpu.VMEM((3, 3, NMAT, PANEL), f32),
            pltpu.VMEM((3, 3, NMAT * SZ, PANEL), bf16),
            pltpu.VMEM((CELLS * SZ, NMAT * SZ), bf16),
            pltpu.VMEM((3, 3, CELLS * SZ, PANEL), bf16),
            pltpu.VMEM(((SX + 2) * (SY + 2), GROUP, PANEL), bf16),
            pltpu.SemaphoreType.DMA,
        ],
        cost_estimate=pl.CostEstimate(flops=2 * ROWS * 21 * PANEL, bytes_accessed=3 * ROWS * PANEL, transcendentals=0),
        compiler_params=pltpu.CompilerParams(vmem_limit_bytes=44 << 20),
        name="local_stencil",
    )(material.transpose(1, 0, 2), blocks.transpose(2, 3, 0, 1), panel, flat)
    tiles = full // HALF
    term = pl.pallas_call(
        edge_kernel,
        in_specs=[vmem] * 2,
        out_specs=vmem,
        out_shape=shape((EDGE, PANEL), f32),
        cost_estimate=pl.CostEstimate(flops=4 * 10**9, bytes_accessed=EDGE * PANEL * 6, transcendentals=0),
        compiler_params=pltpu.CompilerParams(vmem_limit_bytes=8 << 20),
        name="edge_terms",
    )(zface, coef)
    keep, send = pl.pallas_call(
        product_kernel,
        in_specs=[vmem] * 8,
        out_specs=[vmem] * 2,
        out_shape=[shape((tiles, HALF, HALF), dtype) for dtype in (f32, bf16)],
        scratch_shapes=[pltpu.VMEM((ROWS, PANEL), bf16), pltpu.VMEM((PANEL, ROWS), bf16)],
        cost_estimate=pl.CostEstimate(flops=2 * ROWS * full * PANEL, bytes_accessed=2 * ROWS * full, transcendentals=0),
        compiler_params=pltpu.CompilerParams(vmem_limit_bytes=32 << 20),
        name="faces_and_product",
    )(yin, yout, chip, beside, wall, part, term, near)
    mine = (keep + swap(send, "core").astype(f32)).astype(bf16)
    parts = lax.all_to_all(mine.reshape(2 * tiles, HALF // 2, HALF), COL + ("zl",), 0, 0, tiled=True)
    copies = pl.pallas_call(
        near_kernel,
        in_specs=[vmem],
        out_specs=vmem,
        out_shape=shape((16, HALF // 2, HALF), bf16),
        compiler_params=pltpu.CompilerParams(vmem_limit_bytes=4 << 20),
        name="near_sum",
    )(parts)
    planes = lax.all_to_all(copies, Z, 0, 0, tiled=True)
    half = pl.pallas_call(
        fold_kernel,
        in_specs=[vmem],
        out_specs=vmem,
        out_shape=shape((HALF, HALF), f32),
        compiler_params=pltpu.CompilerParams(vmem_limit_bytes=4 << 20),
        name="fold",
    )(planes)
    both = lax.all_gather(half, "core", axis=0, tiled=True)
    return pl.pallas_call(
        flip_kernel,
        in_specs=[vmem],
        out_specs=vmem,
        out_shape=shape((HALF, PANEL), f32),
        compiler_params=pltpu.CompilerParams(vmem_limit_bytes=4 << 20),
        name="flip",
    )(both)


def solution(mesh):
    split = Mesh(mesh.devices.reshape(4, 2, 2, 4, 4, 2), ("zh", "zl", "core", "y", "x", "gz"))
    return jax.shard_map(
        shards,
        mesh=split,
        in_specs=(P(ROW, COL, GZ, None, None), P(), P(ROW, COL, GZ)),
        out_specs=P(COL, None),
        check_vma=False,
    )
```

```python
import jax
import jax.numpy as jnp
from jax import lax
from jax.experimental import pallas as pl
from jax.experimental.pallas import tpu as pltpu
from jax.sharding import Mesh, PartitionSpec as P

PANEL = 256
HALF = 128
NMAT = 8
SX, SY, SZ = 4, 6, 16
CELLS = SX * SY
GROUP = 3 * SZ
ROWS = CELLS * GROUP
EDGE = 3 * CELLS
ROW, COL, GZ = ("zh", "zl", "core"), ("y", "x"), "gz"
Z = ("gz", "zh", "zl")
f32, bf16 = jnp.float32, jnp.bfloat16


def lane(values, o, i, j, width=PANEL):
    k = (3 * i + j) * 7 + o
    return jnp.broadcast_to(values[:, k : k + 1], (values.shape[0], width))


def collect_kernel(modes_ref, panel_ref, z_ref, xin_ref, xout_ref, yin_ref, yout_ref, raw_ref, edge_ref, sem):
    copy = pltpu.make_async_copy(modes_ref.at[:, :PANEL], raw_ref, sem)
    copy.start()
    copy.wait()
    first = jnp.where(lax.axis_index(GZ) == 0, SZ - 1, 0)
    for h in range(2):
        part = slice(h * HALF, (h + 1) * HALF)
        panel_ref[h] = raw_ref[:, part].astype(f32)
        for j in range(3):
            rows = panel_ref.at[h][pl.ds(j * SZ + first, CELLS, stride=GROUP), :]
            edge_ref[j * CELLS : (j + 1) * CELLS, part] = rows
    z_ref[...] = edge_ref[...].astype(bf16)
    side = SY * GROUP
    low = lax.axis_index("core") == 0
    xin_ref[...] = jnp.where(low, raw_ref[ROWS - side :, :], raw_ref[:side, :])
    xout_ref[...] = jnp.where(low, raw_ref[:side, :], raw_ref[ROWS - side :, :])
    even = lax.axis_index("x") % 2 == 0
    for x in range(SX):
        near = raw_ref[x * side : x * side + GROUP, :]
        far = raw_ref[(x + 1) * side - GROUP : (x + 1) * side, :]
        yin_ref[x * GROUP : (x + 1) * GROUP, :] = jnp.where(even, far, near)
        yout_ref[x * GROUP : (x + 1) * GROUP, :] = jnp.where(even, near, far)


def split3(value):
    high = value.astype(bf16).astype(f32)
    mid = (value - high).astype(bf16).astype(f32)
    return high, mid, value - high - mid


def stack3(value):
    return jnp.concatenate([*split3(value), jnp.zeros_like(value)]).astype(bf16)


def local_kernel(kind_ref, blocks_ref, panel_ref, modes_ref,
                 coef_ref, wall_ref, part_ref, near_ref,
                 table_ref, wide_ref, hot_ref, text_ref, weight_ref, place_ref, matrix_ref, grid_ref, sem):
    copy = pltpu.make_async_copy(modes_ref, near_ref, sem)
    copy.start()
    table_ref[...] = jnp.zeros((NMAT, 128), f32)
    text_ref[...] = jnp.zeros(text_ref.shape, f32)
    for i in range(3):
        for j in range(3):
            k = 3 * i + j
            values = blocks_ref[i, j]
            table_ref[:, 7 * k : 7 * k + 7] = values
            for o in range(7):
                column = jnp.broadcast_to(values[:, o : o + 1], (NMAT, HALF))
                own, at = (0, o * GROUP) if o < 5 else (o - 4, 0)
                at += j * SZ
                text_ref[own, i, :, at : at + SZ] = column[:, :SZ]
                if 1 <= o <= 4:
                    wide_ref[o - 1, :, k * HALF : (k + 1) * HALF] = stack3(column)
    row = lax.broadcasted_iota(jnp.int32, (SZ, PANEL), 0)
    column = lax.broadcasted_iota(jnp.int32, (SZ, PANEL), 1)
    same = column % SZ == row
    above = (column % SZ == row + 1) & (column < GROUP)
    below = (column % SZ == row - 1) & (column < GROUP)
    for i in range(3):
        for m in range(NMAT):
            here, up, down = [jnp.broadcast_to(text_ref[own, i, m : m + 1, :], (SZ, PANEL)) for own in range(3)]
            value = jnp.where(same, here, jnp.where(above, up, jnp.where(below, down, 0.0)))
            for part, piece in enumerate(split3(value)):
                weight_ref[part, i, m * SZ : (m + 1) * SZ, :] = piece.astype(bf16)
    kinds = jnp.concatenate([kind_ref[y] for y in range(SY)]).astype(f32).T
    slot = lax.broadcasted_iota(jnp.int32, (SZ, 4 * NMAT), 1)
    slot = jnp.where(slot < 3 * NMAT, slot % NMAT, -1).astype(f32)
    spot = column[:, :128]
    spot = jnp.where(spot % SZ == row[:, :128], spot // SZ, -1).astype(f32)
    none = jnp.zeros((GROUP, PANEL), bf16)
    for n in range(CELLS):
        x, y = divmod(n, SY)
        kind = jnp.broadcast_to(kinds[:, y * SX + x : y * SX + x + 1], (SZ, 128))
        here = slice(n * SZ, (n + 1) * SZ)
        hot_ref[here, :] = jnp.where(kind[:, : 4 * NMAT] == slot, 1.0, 0.0).astype(bf16)
        place_ref[here, :] = jnp.where(kind == spot, 1.0, 0.0).astype(bf16)
        rows = [panel_ref[h, n * GROUP : (n + 1) * GROUP, :] for h in range(2)]
        grid_ref[(x + 1) * (SY + 2) + y + 1] = jnp.concatenate(rows, axis=1).astype(bf16)
    for y in range(SY + 2):
        grid_ref[y] = none
        grid_ref[(SX + 1) * (SY + 2) + y] = none
    for x in range(1, SX + 1):
        grid_ref[x * (SY + 2)] = none
        grid_ref[x * (SY + 2) + SY + 1] = none
    coef_ref[...] = jnp.dot(hot_ref[...], stack3(table_ref[...]), preferred_element_type=f32)
    walls = (
        [(SX - 1) * SY + y for y in range(SY)],
        [y for y in range(SY)],
        [x * SY + SY - 1 for x in range(SX)],
        [x * SY for x in range(SX)],
    )
    for o, cells in enumerate(walls):
        rows = jnp.concatenate([hot_ref[n * SZ : (n + 1) * SZ, :] for n in cells])
        wall_ref[o, : len(cells) * SZ, :] = jnp.dot(rows, wide_ref[o], preferred_element_type=f32)
    for i in range(3):
        for part in range(3):
            product = jnp.dot(place_ref[...], weight_ref[part, i], preferred_element_type=f32)
            matrix_ref[part, i] = product.astype(bf16)
    pad = jnp.zeros((SZ, PANEL), bf16)
    for n in range(CELLS):
        at = (n // SY + 1) * (SY + 2) + n % SY + 1
        here = slice(n * SZ, (n + 1) * SZ)
        left = jnp.concatenate([matrix_ref[part, i, here, :] for part in range(3) for i in range(3)])
        right = jnp.concatenate([grid_ref[k] for k in (at, at + SY + 2, at - SY - 2, at + 1, at - 1)] + [pad])
        out = jnp.dot(left, right, preferred_element_type=f32)
        part_ref[n * GROUP : (n + 1) * GROUP, :] = (out[2 * GROUP :] + out[GROUP : 2 * GROUP]) + out[:GROUP]
    copy.wait()


def edge_kernel(zface_ref, coef_ref, term_ref):
    gz = lax.axis_index(GZ)
    coef = coef_ref[pl.ds(jnp.where(gz == 0, SZ - 1, 0), CELLS, stride=SZ), :]
    coef = jnp.where(gz == 0, coef, pltpu.roll(coef, 127, 1))
    for i in range(3):
        total = jnp.zeros((CELLS, PANEL), f32)
        for j in range(3):
            total = total + lane(coef, 5, i, j) * zface_ref[j * CELLS : (j + 1) * CELLS, :].astype(f32)
        term_ref[i * CELLS : (i + 1) * CELLS, :] = total


def product_kernel(yin_ref, yout_ref, beside_ref, chip_ref, wall_ref, part_ref, term_ref, modes_ref,
                   keep_ref, send_ref, stiff_ref, left_ref):
    core, gz = lax.axis_index("core"), lax.axis_index(GZ)
    level = lax.broadcasted_iota(jnp.int32, (SZ, PANEL), 0)
    at_edge = level == jnp.where(gz == 0, SZ - 1, 0)
    low = core == 0
    even = lax.axis_index("x") % 2 == 0
    for n in range(CELLS):
        x, y = divmod(n, SY)
        faces = [(1, low, chip_ref, beside_ref, y)] if x == SX - 1 else []
        faces += [(2, low, beside_ref, chip_ref, y)] if x == 0 else []
        faces += [(3, even, yin_ref, yout_ref, x)] if y == SY - 1 else []
        faces += [(4, even, yout_ref, yin_ref, x)] if y == 0 else []
        for i in range(3):
            start = n * GROUP + i * SZ
            row = i * CELLS + n
            term = jnp.broadcast_to(term_ref[row : row + 1, :], (SZ, PANEL))
            total = part_ref[start : start + SZ, :] + jnp.where(at_edge, term, 0.0)
            for o, pick, one, two, cell in faces:
                for j in range(3):
                    at = slice(cell * GROUP + j * SZ, cell * GROUP + (j + 1) * SZ)
                    value = jnp.where(pick, one[at, :].astype(f32), two[at, :].astype(f32))
                    k = 3 * i + j
                    factor = wall_ref[o - 1, cell * SZ : (cell + 1) * SZ, k * HALF : (k + 1) * HALF]
                    total = total + jnp.concatenate([factor, factor], axis=1) * value
            stiff_ref[start : start + SZ, :] = total.astype(bf16)
    left_ref[...] = stiff_ref[...].T
    for t in range(modes_ref.shape[1] // PANEL):
        part = slice(t * PANEL, (t + 1) * PANEL)
        product = jnp.dot(left_ref[...], modes_ref[:, part], preferred_element_type=f32)
        low, high = product[:HALF], product[HALF:]
        keep = jnp.where(core == 0, low, high)
        send = jnp.where(core == 0, high, low).astype(bf16)
        for u in range(2):
            keep_ref[2 * t + u] = keep[:, u * HALF : (u + 1) * HALF]
            send_ref[2 * t + u] = send[:, u * HALF : (u + 1) * HALF]


def near_kernel(parts_ref, copies_ref):
    total = parts_ref[0].astype(f32)
    for k in range(1, parts_ref.shape[0]):
        total = total + parts_ref[k].astype(f32)
    total = total.astype(bf16)
    for k in range(copies_ref.shape[0]):
        copies_ref[k] = total


def fold_kernel(planes_ref, half_ref):
    for r in range(2):
        total = planes_ref[r].astype(f32)
        for q in range(1, 8):
            total = total + planes_ref[2 * q + r].astype(f32)
        half_ref[64 * r : 64 * (r + 1), :] = total


def flip_kernel(both_ref, out_ref):
    out_ref[...] = both_ref[...].T


def swap(value, axis):
    return lax.ppermute(value, axis, [(0, 1), (1, 0)])


def shards(modes, blocks, material):
    full = modes.shape[-1]
    flat = modes.transpose(0, 1, 3, 2, 4).reshape(ROWS, full)
    vmem = pl.BlockSpec(memory_space=pltpu.VMEM)
    shape = jax.ShapeDtypeStruct
    xside, yside = SY * GROUP, SX * GROUP
    panel, zsend, xinner, xouter, yinner, youter = pl.pallas_call(
        collect_kernel,
        in_specs=[pl.BlockSpec(memory_space=pl.ANY)],
        out_specs=[vmem] * 6,
        out_shape=[shape((2, ROWS, HALF), f32)]
        + [shape((rows, PANEL), bf16) for rows in (3 * CELLS, xside, xside, yside, yside)],
        scratch_shapes=[pltpu.VMEM((ROWS, PANEL), bf16), pltpu.VMEM((EDGE, PANEL), f32), pltpu.SemaphoreType.DMA],
        compiler_params=pltpu.CompilerParams(vmem_limit_bytes=50 << 20),
        name="collect_faces",
    )(flat)
    zface = swap(zsend, GZ)

    def pairs(start):
        ends = [(i, i + 1) for i in range(start, 15, 2)]
        return ends + [(j, i) for i, j in ends]

    yin = lax.ppermute(yinner, COL, pairs(0))
    yout = lax.ppermute(youter, COL, pairs(1))
    beside = lax.ppermute(xouter, ROW, pairs(1))
    chip = swap(xinner, "core")
    coef, wall, part, near = pl.pallas_call(
        local_kernel,
        in_specs=[vmem] * 3 + [pl.BlockSpec(memory_space=pl.ANY)],
        out_specs=[vmem] * 4,
        out_shape=[shape((CELLS * SZ, 128), f32), shape((4, SY * SZ, 9 * HALF), f32), shape((ROWS, PANEL), f32), shape((ROWS, full), bf16)],
        scratch_shapes=[
            pltpu.VMEM((NMAT, 128), f32),
            pltpu.VMEM((4, 4 * NMAT, 9 * HALF), bf16),
            pltpu.VMEM((CELLS * SZ, 4 * NMAT), bf16),
            pltpu.VMEM((3, 3, NMAT, PANEL), f32),
            pltpu.VMEM((3, 3, NMAT * SZ, PANEL), bf16),
            pltpu.VMEM((CELLS * SZ, NMAT * SZ), bf16),
            pltpu.VMEM((3, 3, CELLS * SZ, PANEL), bf16),
            pltpu.VMEM(((SX + 2) * (SY + 2), GROUP, PANEL), bf16),
            pltpu.SemaphoreType.DMA,
        ],
        cost_estimate=pl.CostEstimate(flops=2 * ROWS * 21 * PANEL, bytes_accessed=3 * ROWS * PANEL, transcendentals=0),
        compiler_params=pltpu.CompilerParams(vmem_limit_bytes=44 << 20),
        name="local_stencil",
    )(material.transpose(1, 0, 2), blocks.transpose(2, 3, 0, 1), panel, flat)
    tiles = full // HALF
    term = pl.pallas_call(
        edge_kernel,
        in_specs=[vmem] * 2,
        out_specs=vmem,
        out_shape=shape((EDGE, PANEL), f32),
        cost_estimate=pl.CostEstimate(flops=4 * 10**9, bytes_accessed=EDGE * PANEL * 6, transcendentals=0),
        compiler_params=pltpu.CompilerParams(vmem_limit_bytes=8 << 20),
        name="edge_terms",
    )(zface, coef)
    keep, send = pl.pallas_call(
        product_kernel,
        in_specs=[vmem] * 8,
        out_specs=[vmem] * 2,
        out_shape=[shape((tiles, HALF, HALF), dtype) for dtype in (f32, bf16)],
        scratch_shapes=[pltpu.VMEM((ROWS, PANEL), bf16), pltpu.VMEM((PANEL, ROWS), bf16)],
        cost_estimate=pl.CostEstimate(flops=2 * ROWS * full * PANEL, bytes_accessed=2 * ROWS * full, transcendentals=0),
        compiler_params=pltpu.CompilerParams(vmem_limit_bytes=32 << 20),
        name="faces_and_product",
    )(yin, yout, beside, chip, wall, part, term, near)
    mine = (keep + swap(send, "core").astype(f32)).astype(bf16)
    parts = lax.all_to_all(mine.reshape(2 * tiles, HALF // 2, HALF), COL + ("zl",), 0, 0, tiled=True)
    copies = pl.pallas_call(
        near_kernel,
        in_specs=[vmem],
        out_specs=vmem,
        out_shape=shape((16, HALF // 2, HALF), bf16),
        compiler_params=pltpu.CompilerParams(vmem_limit_bytes=4 << 20),
        name="near_sum",
    )(parts)
    planes = lax.all_to_all(copies, Z, 0, 0, tiled=True)
    half = pl.pallas_call(
        fold_kernel,
        in_specs=[vmem],
        out_specs=vmem,
        out_shape=shape((HALF, HALF), f32),
        compiler_params=pltpu.CompilerParams(vmem_limit_bytes=4 << 20),
        name="fold",
    )(planes)
    both = lax.all_gather(half, "core", axis=0, tiled=True)
    return pl.pallas_call(
        flip_kernel,
        in_specs=[vmem],
        out_specs=vmem,
        out_shape=shape((HALF, PANEL), f32),
        compiler_params=pltpu.CompilerParams(vmem_limit_bytes=4 << 20),
        name="flip",
    )(both)


def solution(mesh):
    split = Mesh(mesh.devices.reshape(4, 2, 2, 4, 4, 2), ("zh", "zl", "core", "y", "x", "gz"))
    return jax.shard_map(
        shards,
        mesh=split,
        in_specs=(P(ROW, COL, GZ, None, None), P(), P(ROW, COL, GZ)),
        out_specs=P(COL, None),
        check_vma=False,
    )
```

```python
import jax
import jax.numpy as jnp
from jax import lax
from jax.experimental import pallas as pl
from jax.experimental.pallas import tpu as pltpu
from jax.sharding import Mesh, PartitionSpec as P

PANEL = 256
HALF = 128
NMAT = 8
SX, SY, SZ = 4, 6, 16
CELLS = SX * SY
GROUP = 3 * SZ
ROWS = CELLS * GROUP
EDGE = 3 * CELLS
ROW, COL, GZ = ("zh", "zl", "core"), ("y", "x"), "gz"
Z = ("gz", "zh", "zl")
f32, bf16 = jnp.float32, jnp.bfloat16


def lane(values, o, i, j, width=PANEL):
    k = (3 * i + j) * 7 + o
    return jnp.broadcast_to(values[:, k : k + 1], (values.shape[0], width))


def collect_kernel(modes_ref, panel_ref, z_ref, xin_ref, xout_ref, yin_ref, yout_ref, raw_ref, edge_ref, sem):
    copy = pltpu.make_async_copy(modes_ref.at[:, :PANEL], raw_ref, sem)
    copy.start()
    copy.wait()
    first = jnp.where(lax.axis_index(GZ) == 0, SZ - 1, 0)
    for h in range(2):
        part = slice(h * HALF, (h + 1) * HALF)
        panel_ref[h] = raw_ref[:, part].astype(f32)
        for j in range(3):
            rows = panel_ref.at[h][pl.ds(j * SZ + first, CELLS, stride=GROUP), :]
            edge_ref[j * CELLS : (j + 1) * CELLS, part] = rows
    z_ref[...] = edge_ref[...].astype(bf16)
    side = SY * GROUP
    low = lax.axis_index("core") == 0
    xin_ref[...] = jnp.where(low, raw_ref[ROWS - side :, :], raw_ref[:side, :])
    xout_ref[...] = jnp.where(low, raw_ref[:side, :], raw_ref[ROWS - side :, :])
    even = lax.axis_index("x") % 2 == 0
    for x in range(SX):
        near = raw_ref[x * side : x * side + GROUP, :]
        far = raw_ref[(x + 1) * side - GROUP : (x + 1) * side, :]
        yin_ref[x * GROUP : (x + 1) * GROUP, :] = jnp.where(even, far, near)
        yout_ref[x * GROUP : (x + 1) * GROUP, :] = jnp.where(even, near, far)


def split3(value):
    high = value.astype(bf16).astype(f32)
    mid = (value - high).astype(bf16).astype(f32)
    return high, mid, value - high - mid


def stack3(value):
    return jnp.concatenate([*split3(value), jnp.zeros_like(value)]).astype(bf16)


def local_kernel(kind_ref, blocks_ref, panel_ref, modes_ref,
                 coef_ref, wall_ref, part_ref, near_ref,
                 table_ref, wide_ref, hot_ref, text_ref, weight_ref, place_ref, matrix_ref, grid_ref, sem):
    copy = pltpu.make_async_copy(modes_ref, near_ref, sem)
    copy.start()
    table_ref[...] = jnp.zeros((NMAT, 128), f32)
    text_ref[...] = jnp.zeros(text_ref.shape, f32)
    for i in range(3):
        for j in range(3):
            k = 3 * i + j
            values = blocks_ref[i, j]
            table_ref[:, 7 * k : 7 * k + 7] = values
            for o in range(7):
                column = jnp.broadcast_to(values[:, o : o + 1], (NMAT, HALF))
                own, at = (0, o * GROUP) if o < 5 else (o - 4, 0)
                at += j * SZ
                text_ref[own, i, :, at : at + SZ] = column[:, :SZ]
                if 1 <= o <= 4:
                    wide_ref[o - 1, :, k * HALF : (k + 1) * HALF] = stack3(column)
    row = lax.broadcasted_iota(jnp.int32, (SZ, PANEL), 0)
    column = lax.broadcasted_iota(jnp.int32, (SZ, PANEL), 1)
    same = column % SZ == row
    above = (column % SZ == row + 1) & (column < GROUP)
    below = (column % SZ == row - 1) & (column < GROUP)
    for i in range(3):
        for m in range(NMAT):
            here, up, down = [jnp.broadcast_to(text_ref[own, i, m : m + 1, :], (SZ, PANEL)) for own in range(3)]
            value = jnp.where(same, here, jnp.where(above, up, jnp.where(below, down, 0.0)))
            for part, piece in enumerate(split3(value)):
                weight_ref[part, i, m * SZ : (m + 1) * SZ, :] = piece.astype(bf16)
    kinds = jnp.concatenate([kind_ref[y] for y in range(SY)]).astype(f32).T
    slot = lax.broadcasted_iota(jnp.int32, (SZ, 4 * NMAT), 1)
    slot = jnp.where(slot < 3 * NMAT, slot % NMAT, -1).astype(f32)
    spot = column[:, :128]
    spot = jnp.where(spot % SZ == row[:, :128], spot // SZ, -1).astype(f32)
    none = jnp.zeros((GROUP, PANEL), bf16)
    for n in range(CELLS):
        x, y = divmod(n, SY)
        kind = jnp.broadcast_to(kinds[:, y * SX + x : y * SX + x + 1], (SZ, 128))
        here = slice(n * SZ, (n + 1) * SZ)
        hot_ref[here, :] = jnp.where(kind[:, : 4 * NMAT] == slot, 1.0, 0.0).astype(bf16)
        place_ref[here, :] = jnp.where(kind == spot, 1.0, 0.0).astype(bf16)
        rows = [panel_ref[h, n * GROUP : (n + 1) * GROUP, :] for h in range(2)]
        grid_ref[(x + 1) * (SY + 2) + y + 1] = jnp.concatenate(rows, axis=1).astype(bf16)
    for y in range(SY + 2):
        grid_ref[y] = none
        grid_ref[(SX + 1) * (SY + 2) + y] = none
    for x in range(1, SX + 1):
        grid_ref[x * (SY + 2)] = none
        grid_ref[x * (SY + 2) + SY + 1] = none
    coef_ref[...] = jnp.dot(hot_ref[...], stack3(table_ref[...]), preferred_element_type=f32)
    walls = (
        [(SX - 1) * SY + y for y in range(SY)],
        [y for y in range(SY)],
        [x * SY + SY - 1 for x in range(SX)],
        [x * SY for x in range(SX)],
    )
    for o, cells in enumerate(walls):
        rows = jnp.concatenate([hot_ref[n * SZ : (n + 1) * SZ, :] for n in cells])
        wall_ref[o, : len(cells) * SZ, :] = jnp.dot(rows, wide_ref[o], preferred_element_type=f32)
    for i in range(3):
        for part in range(3):
            product = jnp.dot(place_ref[...], weight_ref[part, i], preferred_element_type=f32)
            matrix_ref[part, i] = product.astype(bf16)
    pad = jnp.zeros((SZ, PANEL), bf16)
    for n in range(CELLS):
        at = (n // SY + 1) * (SY + 2) + n % SY + 1
        here = slice(n * SZ, (n + 1) * SZ)
        left = jnp.concatenate([matrix_ref[part, i, here, :] for part in range(3) for i in range(3)])
        right = jnp.concatenate([grid_ref[k] for k in (at, at + SY + 2, at - SY - 2, at + 1, at - 1)] + [pad])
        out = jnp.dot(left, right, preferred_element_type=f32)
        part_ref[n * GROUP : (n + 1) * GROUP, :] = (out[2 * GROUP :] + out[GROUP : 2 * GROUP]) + out[:GROUP]
    copy.wait()


def edge_kernel(zface_ref, coef_ref, term_ref):
    gz = lax.axis_index(GZ)
    coef = coef_ref[pl.ds(jnp.where(gz == 0, SZ - 1, 0), CELLS, stride=SZ), :]
    coef = jnp.where(gz == 0, coef, pltpu.roll(coef, 127, 1))
    for i in range(3):
        total = jnp.zeros((CELLS, PANEL), f32)
        for j in range(3):
            total = total + lane(coef, 5, i, j) * zface_ref[j * CELLS : (j + 1) * CELLS, :].astype(f32)
        term_ref[i * CELLS : (i + 1) * CELLS, :] = total


def product_kernel(yout_ref, yin_ref, beside_ref, chip_ref, wall_ref, part_ref, term_ref, modes_ref,
                   keep_ref, send_ref, stiff_ref, left_ref):
    core, gz = lax.axis_index("core"), lax.axis_index(GZ)
    level = lax.broadcasted_iota(jnp.int32, (SZ, PANEL), 0)
    at_edge = level == jnp.where(gz == 0, SZ - 1, 0)
    low = core == 0
    even = lax.axis_index("x") % 2 == 0
    for n in range(CELLS):
        x, y = divmod(n, SY)
        faces = [(1, low, chip_ref, beside_ref, y)] if x == SX - 1 else []
        faces += [(2, low, beside_ref, chip_ref, y)] if x == 0 else []
        faces += [(3, even, yin_ref, yout_ref, x)] if y == SY - 1 else []
        faces += [(4, even, yout_ref, yin_ref, x)] if y == 0 else []
        for i in range(3):
            start = n * GROUP + i * SZ
            row = i * CELLS + n
            term = jnp.broadcast_to(term_ref[row : row + 1, :], (SZ, PANEL))
            total = part_ref[start : start + SZ, :] + jnp.where(at_edge, term, 0.0)
            for o, pick, one, two, cell in faces:
                for j in range(3):
                    at = slice(cell * GROUP + j * SZ, cell * GROUP + (j + 1) * SZ)
                    value = jnp.where(pick, one[at, :].astype(f32), two[at, :].astype(f32))
                    k = 3 * i + j
                    factor = wall_ref[o - 1, cell * SZ : (cell + 1) * SZ, k * HALF : (k + 1) * HALF]
                    total = total + jnp.concatenate([factor, factor], axis=1) * value
            stiff_ref[start : start + SZ, :] = total.astype(bf16)
    left_ref[...] = stiff_ref[...].T
    for t in range(modes_ref.shape[1] // PANEL):
        part = slice(t * PANEL, (t + 1) * PANEL)
        product = jnp.dot(left_ref[...], modes_ref[:, part], preferred_element_type=f32)
        low, high = product[:HALF], product[HALF:]
        keep = jnp.where(core == 0, low, high)
        send = jnp.where(core == 0, high, low).astype(bf16)
        for u in range(2):
            keep_ref[2 * t + u] = keep[:, u * HALF : (u + 1) * HALF]
            send_ref[2 * t + u] = send[:, u * HALF : (u + 1) * HALF]


def near_kernel(parts_ref, copies_ref):
    total = parts_ref[0].astype(f32)
    for k in range(1, parts_ref.shape[0]):
        total = total + parts_ref[k].astype(f32)
    total = total.astype(bf16)
    for k in range(copies_ref.shape[0]):
        copies_ref[k] = total


def fold_kernel(planes_ref, half_ref):
    for r in range(2):
        total = planes_ref[r].astype(f32)
        for q in range(1, 8):
            total = total + planes_ref[2 * q + r].astype(f32)
        half_ref[64 * r : 64 * (r + 1), :] = total


def flip_kernel(both_ref, out_ref):
    out_ref[...] = both_ref[...].T


def swap(value, axis):
    return lax.ppermute(value, axis, [(0, 1), (1, 0)])


def shards(modes, blocks, material):
    full = modes.shape[-1]
    flat = modes.transpose(0, 1, 3, 2, 4).reshape(ROWS, full)
    vmem = pl.BlockSpec(memory_space=pltpu.VMEM)
    shape = jax.ShapeDtypeStruct
    xside, yside = SY * GROUP, SX * GROUP
    panel, zsend, xinner, xouter, yinner, youter = pl.pallas_call(
        collect_kernel,
        in_specs=[pl.BlockSpec(memory_space=pl.ANY)],
        out_specs=[vmem] * 6,
        out_shape=[shape((2, ROWS, HALF), f32)]
        + [shape((rows, PANEL), bf16) for rows in (3 * CELLS, xside, xside, yside, yside)],
        scratch_shapes=[pltpu.VMEM((ROWS, PANEL), bf16), pltpu.VMEM((EDGE, PANEL), f32), pltpu.SemaphoreType.DMA],
        compiler_params=pltpu.CompilerParams(vmem_limit_bytes=50 << 20),
        name="collect_faces",
    )(flat)
    zface = swap(zsend, GZ)

    def pairs(start):
        ends = [(i, i + 1) for i in range(start, 15, 2)]
        return ends + [(j, i) for i, j in ends]

    yin = lax.ppermute(yinner, COL, pairs(0))
    yout = lax.ppermute(youter, COL, pairs(1))
    beside = lax.ppermute(xouter, ROW, pairs(1))
    chip = swap(xinner, "core")
    coef, wall, part, near = pl.pallas_call(
        local_kernel,
        in_specs=[vmem] * 3 + [pl.BlockSpec(memory_space=pl.ANY)],
        out_specs=[vmem] * 4,
        out_shape=[shape((CELLS * SZ, 128), f32), shape((4, SY * SZ, 9 * HALF), f32), shape((ROWS, PANEL), f32), shape((ROWS, full), bf16)],
        scratch_shapes=[
            pltpu.VMEM((NMAT, 128), f32),
            pltpu.VMEM((4, 4 * NMAT, 9 * HALF), bf16),
            pltpu.VMEM((CELLS * SZ, 4 * NMAT), bf16),
            pltpu.VMEM((3, 3, NMAT, PANEL), f32),
            pltpu.VMEM((3, 3, NMAT * SZ, PANEL), bf16),
            pltpu.VMEM((CELLS * SZ, NMAT * SZ), bf16),
            pltpu.VMEM((3, 3, CELLS * SZ, PANEL), bf16),
            pltpu.VMEM(((SX + 2) * (SY + 2), GROUP, PANEL), bf16),
            pltpu.SemaphoreType.DMA,
        ],
        cost_estimate=pl.CostEstimate(flops=2 * ROWS * 21 * PANEL, bytes_accessed=3 * ROWS * PANEL, transcendentals=0),
        compiler_params=pltpu.CompilerParams(vmem_limit_bytes=44 << 20),
        name="local_stencil",
    )(material.transpose(1, 0, 2), blocks.transpose(2, 3, 0, 1), panel, flat)
    tiles = full // HALF
    term = pl.pallas_call(
        edge_kernel,
        in_specs=[vmem] * 2,
        out_specs=vmem,
        out_shape=shape((EDGE, PANEL), f32),
        cost_estimate=pl.CostEstimate(flops=4 * 10**9, bytes_accessed=EDGE * PANEL * 6, transcendentals=0),
        compiler_params=pltpu.CompilerParams(vmem_limit_bytes=8 << 20),
        name="edge_terms",
    )(zface, coef)
    keep, send = pl.pallas_call(
        product_kernel,
        in_specs=[vmem] * 8,
        out_specs=[vmem] * 2,
        out_shape=[shape((tiles, HALF, HALF), dtype) for dtype in (f32, bf16)],
        scratch_shapes=[pltpu.VMEM((ROWS, PANEL), bf16), pltpu.VMEM((PANEL, ROWS), bf16)],
        cost_estimate=pl.CostEstimate(flops=2 * ROWS * full * PANEL, bytes_accessed=2 * ROWS * full, transcendentals=0),
        compiler_params=pltpu.CompilerParams(vmem_limit_bytes=32 << 20),
        name="faces_and_product",
    )(yout, yin, beside, chip, wall, part, term, near)
    mine = (keep + swap(send, "core").astype(f32)).astype(bf16)
    parts = lax.all_to_all(mine.reshape(2 * tiles, HALF // 2, HALF), COL + ("zl",), 0, 0, tiled=True)
    copies = pl.pallas_call(
        near_kernel,
        in_specs=[vmem],
        out_specs=vmem,
        out_shape=shape((16, HALF // 2, HALF), bf16),
        compiler_params=pltpu.CompilerParams(vmem_limit_bytes=4 << 20),
        name="near_sum",
    )(parts)
    planes = lax.all_to_all(copies, Z, 0, 0, tiled=True)
    half = pl.pallas_call(
        fold_kernel,
        in_specs=[vmem],
        out_specs=vmem,
        out_shape=shape((HALF, HALF), f32),
        compiler_params=pltpu.CompilerParams(vmem_limit_bytes=4 << 20),
        name="fold",
    )(planes)
    both = lax.all_gather(half, "core", axis=0, tiled=True)
    return pl.pallas_call(
        flip_kernel,
        in_specs=[vmem],
        out_specs=vmem,
        out_shape=shape((HALF, PANEL), f32),
        compiler_params=pltpu.CompilerParams(vmem_limit_bytes=4 << 20),
        name="flip",
    )(both)


def solution(mesh):
    split = Mesh(mesh.devices.reshape(4, 2, 2, 4, 4, 2), ("zh", "zl", "core", "y", "x", "gz"))
    return jax.shard_map(
        shards,
        mesh=split,
        in_specs=(P(ROW, COL, GZ, None, None), P(), P(ROW, COL, GZ)),
        out_specs=P(COL, None),
        check_vma=False,
    )
```

```python
import jax
import jax.numpy as jnp
from jax import lax
from jax.experimental import pallas as pl
from jax.experimental.pallas import tpu as pltpu
from jax.sharding import Mesh, PartitionSpec as P

PANEL = 256
HALF = 128
NMAT = 8
SX, SY, SZ = 4, 6, 16
CELLS = SX * SY
GROUP = 3 * SZ
ROWS = CELLS * GROUP
EDGE = 3 * CELLS
ROW, COL, GZ = ("zh", "zl", "core"), ("y", "x"), "gz"
Z = ("gz", "zh", "zl")
f32, bf16 = jnp.float32, jnp.bfloat16


def lane(values, o, i, j, width=PANEL):
    k = (3 * i + j) * 7 + o
    return jnp.broadcast_to(values[:, k : k + 1], (values.shape[0], width))


def collect_kernel(modes_ref, panel_ref, z_ref, xin_ref, xout_ref, yin_ref, yout_ref, raw_ref, edge_ref, sem):
    copy = pltpu.make_async_copy(modes_ref.at[:, :PANEL], raw_ref, sem)
    copy.start()
    copy.wait()
    first = jnp.where(lax.axis_index(GZ) == 0, SZ - 1, 0)
    for h in range(2):
        part = slice(h * HALF, (h + 1) * HALF)
        panel_ref[h] = raw_ref[:, part].astype(f32)
        for j in range(3):
            rows = panel_ref.at[h][pl.ds(j * SZ + first, CELLS, stride=GROUP), :]
            edge_ref[j * CELLS : (j + 1) * CELLS, part] = rows
    z_ref[...] = edge_ref[...].astype(bf16)
    side = SY * GROUP
    low = lax.axis_index("core") == 0
    xin_ref[...] = jnp.where(low, raw_ref[ROWS - side :, :], raw_ref[:side, :])
    xout_ref[...] = jnp.where(low, raw_ref[:side, :], raw_ref[ROWS - side :, :])
    even = lax.axis_index("x") % 2 == 0
    for x in range(SX):
        near = raw_ref[x * side : x * side + GROUP, :]
        far = raw_ref[(x + 1) * side - GROUP : (x + 1) * side, :]
        yin_ref[x * GROUP : (x + 1) * GROUP, :] = jnp.where(even, far, near)
        yout_ref[x * GROUP : (x + 1) * GROUP, :] = jnp.where(even, near, far)


def split3(value):
    high = value.astype(bf16).astype(f32)
    mid = (value - high).astype(bf16).astype(f32)
    return high, mid, value - high - mid


def stack3(value):
    return jnp.concatenate([*split3(value), jnp.zeros_like(value)]).astype(bf16)


def local_kernel(kind_ref, blocks_ref, panel_ref, modes_ref,
                 coef_ref, wall_ref, part_ref, near_ref,
                 table_ref, wide_ref, hot_ref, text_ref, weight_ref, place_ref, matrix_ref, grid_ref, sem):
    copy = pltpu.make_async_copy(modes_ref, near_ref, sem)
    copy.start()
    table_ref[...] = jnp.zeros((NMAT, 128), f32)
    text_ref[...] = jnp.zeros(text_ref.shape, f32)
    for i in range(3):
        for j in range(3):
            k = 3 * i + j
            values = blocks_ref[i, j]
            table_ref[:, 7 * k : 7 * k + 7] = values
            for o in range(7):
                column = jnp.broadcast_to(values[:, o : o + 1], (NMAT, HALF))
                own, at = (0, o * GROUP) if o < 5 else (o - 4, 0)
                at += j * SZ
                text_ref[own, i, :, at : at + SZ] = column[:, :SZ]
                if 1 <= o <= 4:
                    wide_ref[o - 1, :, k * HALF : (k + 1) * HALF] = stack3(column)
    row = lax.broadcasted_iota(jnp.int32, (SZ, PANEL), 0)
    column = lax.broadcasted_iota(jnp.int32, (SZ, PANEL), 1)
    same = column % SZ == row
    above = (column % SZ == row + 1) & (column < GROUP)
    below = (column % SZ == row - 1) & (column < GROUP)
    for i in range(3):
        for m in range(NMAT):
            here, up, down = [jnp.broadcast_to(text_ref[own, i, m : m + 1, :], (SZ, PANEL)) for own in range(3)]
            value = jnp.where(same, here, jnp.where(above, up, jnp.where(below, down, 0.0)))
            for part, piece in enumerate(split3(value)):
                weight_ref[part, i, m * SZ : (m + 1) * SZ, :] = piece.astype(bf16)
    kinds = jnp.concatenate([kind_ref[y] for y in range(SY)]).astype(f32).T
    slot = lax.broadcasted_iota(jnp.int32, (SZ, 4 * NMAT), 1)
    slot = jnp.where(slot < 3 * NMAT, slot % NMAT, -1).astype(f32)
    spot = column[:, :128]
    spot = jnp.where(spot % SZ == row[:, :128], spot // SZ, -1).astype(f32)
    none = jnp.zeros((GROUP, PANEL), bf16)
    for n in range(CELLS):
        x, y = divmod(n, SY)
        kind = jnp.broadcast_to(kinds[:, y * SX + x : y * SX + x + 1], (SZ, 128))
        here = slice(n * SZ, (n + 1) * SZ)
        hot_ref[here, :] = jnp.where(kind[:, : 4 * NMAT] == slot, 1.0, 0.0).astype(bf16)
        place_ref[here, :] = jnp.where(kind == spot, 1.0, 0.0).astype(bf16)
        rows = [panel_ref[h, n * GROUP : (n + 1) * GROUP, :] for h in range(2)]
        grid_ref[(x + 1) * (SY + 2) + y + 1] = jnp.concatenate(rows, axis=1).astype(bf16)
    for y in range(SY + 2):
        grid_ref[y] = none
        grid_ref[(SX + 1) * (SY + 2) + y] = none
    for x in range(1, SX + 1):
        grid_ref[x * (SY + 2)] = none
        grid_ref[x * (SY + 2) + SY + 1] = none
    coef_ref[...] = jnp.dot(hot_ref[...], stack3(table_ref[...]), preferred_element_type=f32)
    walls = (
        [(SX - 1) * SY + y for y in range(SY)],
        [y for y in range(SY)],
        [x * SY + SY - 1 for x in range(SX)],
        [x * SY for x in range(SX)],
    )
    for o, cells in enumerate(walls):
        rows = jnp.concatenate([hot_ref[n * SZ : (n + 1) * SZ, :] for n in cells])
        wall_ref[o, : len(cells) * SZ, :] = jnp.dot(rows, wide_ref[o], preferred_element_type=f32)
    for i in range(3):
        for part in range(3):
            product = jnp.dot(place_ref[...], weight_ref[part, i], preferred_element_type=f32)
            matrix_ref[part, i] = product.astype(bf16)
    pad = jnp.zeros((SZ, PANEL), bf16)
    for n in range(CELLS):
        at = (n // SY + 1) * (SY + 2) + n % SY + 1
        here = slice(n * SZ, (n + 1) * SZ)
        left = jnp.concatenate([matrix_ref[part, i, here, :] for part in range(3) for i in range(3)])
        right = jnp.concatenate([grid_ref[k] for k in (at, at + SY + 2, at - SY - 2, at + 1, at - 1)] + [pad])
        out = jnp.dot(left, right, preferred_element_type=f32)
        part_ref[n * GROUP : (n + 1) * GROUP, :] = (out[2 * GROUP :] + out[GROUP : 2 * GROUP]) + out[:GROUP]
    copy.wait()


def edge_kernel(zface_ref, coef_ref, term_ref):
    gz = lax.axis_index(GZ)
    coef = coef_ref[pl.ds(jnp.where(gz == 0, SZ - 1, 0), CELLS, stride=SZ), :]
    coef = jnp.where(gz == 0, coef, pltpu.roll(coef, 127, 1))
    for i in range(3):
        total = jnp.zeros((CELLS, PANEL), f32)
        for j in range(3):
            total = total + lane(coef, 5, i, j) * zface_ref[j * CELLS : (j + 1) * CELLS, :].astype(f32)
        term_ref[i * CELLS : (i + 1) * CELLS, :] = total


def product_kernel(yout_ref, yin_ref, beside_ref, chip_ref, wall_ref, part_ref, term_ref, modes_ref,
                   keep_ref, send_ref, stiff_ref, left_ref):
    core, gz = lax.axis_index("core"), lax.axis_index(GZ)
    level = lax.broadcasted_iota(jnp.int32, (SZ, PANEL), 0)
    at_edge = level == jnp.where(gz == 0, SZ - 1, 0)
    low = core == 0
    even = lax.axis_index("x") % 2 == 0
    for n in range(CELLS):
        x, y = divmod(n, SY)
        faces = [(1, low, chip_ref, beside_ref, y)] if x == SX - 1 else []
        faces += [(2, low, beside_ref, chip_ref, y)] if x == 0 else []
        faces += [(3, even, yin_ref, yout_ref, x)] if y == SY - 1 else []
        faces += [(4, even, yout_ref, yin_ref, x)] if y == 0 else []
        for i in range(3):
            start = n * GROUP + i * SZ
            row = i * CELLS + n
            term = jnp.broadcast_to(term_ref[row : row + 1, :], (SZ, PANEL))
            total = part_ref[start : start + SZ, :] + jnp.where(at_edge, term, 0.0)
            for o, pick, one, two, cell in faces:
                for j in range(3):
                    at = slice(cell * GROUP + j * SZ, cell * GROUP + (j + 1) * SZ)
                    value = jnp.where(pick, one[at, :].astype(f32), two[at, :].astype(f32))
                    k = 3 * i + j
                    factor = wall_ref[o - 1, cell * SZ : (cell + 1) * SZ, k * HALF : (k + 1) * HALF]
                    total = total + jnp.concatenate([factor, factor], axis=1) * value
            stiff_ref[start : start + SZ, :] = total.astype(bf16)
    left_ref[...] = stiff_ref[...].T
    for t in range(modes_ref.shape[1] // PANEL):
        part = slice(t * PANEL, (t + 1) * PANEL)
        product = jnp.dot(left_ref[...], modes_ref[:, part], preferred_element_type=f32)
        low, high = product[:HALF], product[HALF:]
        keep = jnp.where(core == 0, low, high)
        send = jnp.where(core == 0, high, low).astype(bf16)
        for u in range(2):
            keep_ref[2 * t + u] = keep[:, u * HALF : (u + 1) * HALF]
            send_ref[2 * t + u] = send[:, u * HALF : (u + 1) * HALF]


def near_kernel(parts_ref, copies_ref):
    total = parts_ref[0].astype(f32)
    for k in range(1, parts_ref.shape[0]):
        total = total + parts_ref[k].astype(f32)
    total = total.astype(bf16)
    for k in range(copies_ref.shape[0]):
        copies_ref[k] = total


def fold_kernel(planes_ref, half_ref):
    for r in range(2):
        total = planes_ref[r].astype(f32)
        for q in range(1, 8):
            total = total + planes_ref[2 * q + r].astype(f32)
        half_ref[:, 64 * r : 64 * (r + 1)] = total.T


def swap(value, axis):
    return lax.ppermute(value, axis, [(0, 1), (1, 0)])


def shards(modes, blocks, material):
    full = modes.shape[-1]
    flat = modes.transpose(0, 1, 3, 2, 4).reshape(ROWS, full)
    vmem = pl.BlockSpec(memory_space=pltpu.VMEM)
    shape = jax.ShapeDtypeStruct
    xside, yside = SY * GROUP, SX * GROUP
    panel, zsend, xinner, xouter, yinner, youter = pl.pallas_call(
        collect_kernel,
        in_specs=[pl.BlockSpec(memory_space=pl.ANY)],
        out_specs=[vmem] * 6,
        out_shape=[shape((2, ROWS, HALF), f32)]
        + [shape((rows, PANEL), bf16) for rows in (3 * CELLS, xside, xside, yside, yside)],
        scratch_shapes=[pltpu.VMEM((ROWS, PANEL), bf16), pltpu.VMEM((EDGE, PANEL), f32), pltpu.SemaphoreType.DMA],
        compiler_params=pltpu.CompilerParams(vmem_limit_bytes=50 << 20),
        name="collect_faces",
    )(flat)
    zface = swap(zsend, GZ)

    def pairs(start):
        ends = [(i, i + 1) for i in range(start, 15, 2)]
        return ends + [(j, i) for i, j in ends]

    yin = lax.ppermute(yinner, COL, pairs(0))
    yout = lax.ppermute(youter, COL, pairs(1))
    beside = lax.ppermute(xouter, ROW, pairs(1))
    chip = swap(xinner, "core")
    coef, wall, part, near = pl.pallas_call(
        local_kernel,
        in_specs=[vmem] * 3 + [pl.BlockSpec(memory_space=pl.ANY)],
        out_specs=[vmem] * 4,
        out_shape=[shape((CELLS * SZ, 128), f32), shape((4, SY * SZ, 9 * HALF), f32), shape((ROWS, PANEL), f32), shape((ROWS, full), bf16)],
        scratch_shapes=[
            pltpu.VMEM((NMAT, 128), f32),
            pltpu.VMEM((4, 4 * NMAT, 9 * HALF), bf16),
            pltpu.VMEM((CELLS * SZ, 4 * NMAT), bf16),
            pltpu.VMEM((3, 3, NMAT, PANEL), f32),
            pltpu.VMEM((3, 3, NMAT * SZ, PANEL), bf16),
            pltpu.VMEM((CELLS * SZ, NMAT * SZ), bf16),
            pltpu.VMEM((3, 3, CELLS * SZ, PANEL), bf16),
            pltpu.VMEM(((SX + 2) * (SY + 2), GROUP, PANEL), bf16),
            pltpu.SemaphoreType.DMA,
        ],
        cost_estimate=pl.CostEstimate(flops=2 * ROWS * 21 * PANEL, bytes_accessed=3 * ROWS * PANEL, transcendentals=0),
        compiler_params=pltpu.CompilerParams(vmem_limit_bytes=44 << 20),
        name="local_stencil",
    )(material.transpose(1, 0, 2), blocks.transpose(2, 3, 0, 1), panel, flat)
    tiles = full // HALF
    term = pl.pallas_call(
        edge_kernel,
        in_specs=[vmem] * 2,
        out_specs=vmem,
        out_shape=shape((EDGE, PANEL), f32),
        cost_estimate=pl.CostEstimate(flops=4 * 10**9, bytes_accessed=EDGE * PANEL * 6, transcendentals=0),
        compiler_params=pltpu.CompilerParams(vmem_limit_bytes=8 << 20),
        name="edge_terms",
    )(zface, coef)
    keep, send = pl.pallas_call(
        product_kernel,
        in_specs=[vmem] * 8,
        out_specs=[vmem] * 2,
        out_shape=[shape((tiles, HALF, HALF), dtype) for dtype in (f32, bf16)],
        scratch_shapes=[pltpu.VMEM((ROWS, PANEL), bf16), pltpu.VMEM((PANEL, ROWS), bf16)],
        cost_estimate=pl.CostEstimate(flops=2 * ROWS * full * PANEL, bytes_accessed=2 * ROWS * full, transcendentals=0),
        compiler_params=pltpu.CompilerParams(vmem_limit_bytes=32 << 20),
        name="faces_and_product",
    )(yout, yin, beside, chip, wall, part, term, near)
    mine = (keep + swap(send, "core").astype(f32)).astype(bf16)
    parts = lax.all_to_all(mine.reshape(2 * tiles, HALF // 2, HALF), COL + ("zl",), 0, 0, tiled=True)
    copies = pl.pallas_call(
        near_kernel,
        in_specs=[vmem],
        out_specs=vmem,
        out_shape=shape((16, HALF // 2, HALF), bf16),
        compiler_params=pltpu.CompilerParams(vmem_limit_bytes=4 << 20),
        name="near_sum",
    )(parts)
    planes = lax.all_to_all(copies, Z, 0, 0, tiled=True)
    half = pl.pallas_call(
        fold_kernel,
        in_specs=[vmem],
        out_specs=vmem,
        out_shape=shape((HALF, HALF), f32),
        compiler_params=pltpu.CompilerParams(vmem_limit_bytes=4 << 20),
        name="fold",
    )(planes)
    strips = half.reshape(HALF // 8, 1, 8, HALF)
    both = lax.all_gather(strips, "core", axis=1, tiled=True)
    return both.transpose(0, 2, 1, 3).reshape(HALF, PANEL)


def solution(mesh):
    split = Mesh(mesh.devices.reshape(4, 2, 2, 4, 4, 2), ("zh", "zl", "core", "y", "x", "gz"))
    return jax.shard_map(
        shards,
        mesh=split,
        in_specs=(P(ROW, COL, GZ, None, None), P(), P(ROW, COL, GZ)),
        out_specs=P(COL, None),
        check_vma=False,
    )
```
